256 devices in a mesh: batch: 2 (over x_hi), head: 8 (over y, x_lo), blk: 16 (over z, core).
Axes of the slice: x: 4 (x_hi: 2, x_lo: 2; x = x_hi * 2 + x_lo), y: 4, z: 8, core: 2. Of those that a mesh axis runs over, the one named last changes fastest.
Arguments:
- tokens: bfloat16 [32, 2048, 1024], P(('batch', 'blk'), 'head'), parts along dimension 0, may hold values from -10.5 to 10.5
- proj_weight: bfloat16 [1024, 3072], replicated, may hold values from -0.1875 to 0.1875
- out_weight: bfloat16 [1024, 1024], replicated, may hold values from -1.5 to 1.5
- pattern: int32 [512, 16], P(('batch', 'blk')), parts along dimension 0, may hold values from 0 to 255, as said below
Outputs:
- mixed_out: bfloat16 [32, 2048, 1024], P(('batch', 'blk'), 'head'), parts along dimension 0
The draws below stay inside these ranges and needn't reach their ends.
There are 2 independent parts, one for each index of `batch`. The reference program is written for one: setup_inputs(seed, part) draws one part's arguments, and reference() takes and returns one part's arrays. A program takes and returns all parts, laid end to end along the dimension named above; an argument that names none is the same for every part. Nothing has to cross between parts.
Inputs may be any that keep to these rules, and one draw needn't show every extreme that they name: `pattern`: row i lists first 6 distinct blocks j with |j - i| <= 8, among them i itself, then 10 distinct summary blocks j (j % 16 >= 12) with |j - i| > 8. Every row with 8 <= i < 248 lists i - 8 and i + 8.
All inputs are finite; a program needn't handle non-finite values.
Results may differ from the reference program's by a relative error of at most 0.0095.
Values may be sent and summed in bfloat16 or wider, within the bound.
A program may use at most 128 MiB of HBM per device.

```python
import jax
import jax.numpy as jnp
from jax import lax

D = 1024
H = 16
HD = 64
BLK = 128
TOK_DEV = 2048
REACH = 8
LSEL = 6
SSEL = 10
SUMB = 4
SB = 16
KSEL = 16
TOKENS = 32768
NBLOCKS = 256
NSUM = 64
N_BLK = 16


def draw_tokens(key, part):
    shape = (N_BLK, TOK_DEV, D)
    keys = jax.random.split(key, 1)
    return jnp.clip(1.25 * jax.random.normal(keys[0], shape, jnp.float32), -7.5, 7.5).astype(jnp.bfloat16)


def draw_proj_weight(key, part):
    weight = jnp.clip(jax.random.normal(key, (D, 3 * D), jnp.float32), -6.0, 6.0) * D ** (-0.5)
    return weight.astype(jnp.bfloat16)


def draw_pattern(key, part):
    keys = jax.random.split(key, 2)
    span = 2 * REACH + 1
    rows = jnp.arange(NBLOCKS, dtype=jnp.int32)[:, None]
    offsets = jnp.arange(span, dtype=jnp.int32)[None, :] - REACH
    target = rows + offsets
    valid = jnp.logical_and(target >= 0, target < NBLOCKS)
    forced = jnp.logical_or(offsets == 0, jnp.logical_or(offsets == -REACH, offsets == REACH))
    column = jnp.arange(span, dtype=jnp.int32)[None, :]
    noise = jax.random.randint(keys[0], (NBLOCKS, span), 0, 2 ** 20)
    ranked = 64 + noise * span + column
    ranked = jnp.where(forced, column, ranked)
    ranked = jnp.where(valid, ranked, 2 ** 30 + column)
    order = jnp.argsort(ranked, axis=1)[:, :LSEL]
    near_ids = jnp.take_along_axis(target, order, axis=1)
    counter = jnp.arange(NSUM, dtype=jnp.int32)
    summary_ids = counter // SUMB * SB + SB - SUMB + counter % SUMB
    too_near = jnp.abs(summary_ids[None, :] - rows) <= REACH
    noise_far = jax.random.randint(keys[1], (NBLOCKS, NSUM), 0, 2 ** 20)
    ranked_far = jnp.where(too_near, 2 ** 30 + counter[None, :], noise_far * NSUM + counter[None, :])
    order_far = jnp.argsort(ranked_far, axis=1)[:, :SSEL]
    far_ids = summary_ids[order_far]
    return jnp.concatenate([near_ids, far_ids], axis=1).astype(jnp.int32)


def scatter_about(key, shape, deviation, bound, kind=jnp.bfloat16):
    entries = deviation * jax.random.normal(key, shape, jnp.float32)
    return jnp.clip(entries, min=-bound, max=bound).astype(kind)


def setup_inputs(seed: int = 0, part: int = 0) -> dict:
    splits = jax.random.split(jax.random.key(seed), 5)
    own_keys = jax.random.split(jax.random.fold_in(splits[4], part), 5)
    return {
        "tokens": draw_tokens(jax.random.fold_in(jax.random.fold_in(splits[4], part), 71), part),
        "proj_weight": draw_proj_weight(jax.random.fold_in(splits[4], 71), part),
        "out_weight": scatter_about(splits[2], (D, D), (8.0 / D ** 0.5), 1.5),
        "pattern": draw_pattern(jax.random.fold_in(jax.random.fold_in(splits[4], part), 71), part),
    }


def attend_block(queries, key_rows, value_rows):
    scores = jnp.einsum("qhe,khe->hqk", queries.astype(jnp.float32), key_rows.astype(jnp.float32)) * (HD ** -0.5)
    row_max = jnp.max(scores, axis=-1, keepdims=True)
    raised = jnp.exp(scores - row_max)
    weights = (raised / jnp.sum(raised, axis=-1, keepdims=True)).astype(jnp.bfloat16)
    result = jnp.einsum("hqk,khe->qhe", weights.astype(jnp.float32), value_rows.astype(jnp.float32))
    return result.astype(jnp.bfloat16)


def reference(tokens, proj_weight, out_weight, pattern):
    flat = tokens.reshape(TOKENS, D)
    projected = jnp.dot(flat, proj_weight, preferred_element_type=jnp.float32).astype(jnp.bfloat16)
    shaped = projected.reshape(NBLOCKS, BLK, H, 3, HD)
    queries = shaped[:, :, :, 0]
    keys_all = shaped[:, :, :, 1]
    values_all = shaped[:, :, :, 2]

    def one_block(index):
        chosen = pattern[index]
        key_rows = keys_all[chosen].reshape(KSEL * BLK, H, HD)
        value_rows = values_all[chosen].reshape(KSEL * BLK, H, HD)
        return attend_block(queries[index], key_rows, value_rows)

    heads = lax.map(one_block, jnp.arange(NBLOCKS, dtype=jnp.int32))
    heads = heads.reshape(TOKENS, D)
    mixed_out = jnp.dot(heads, out_weight, preferred_element_type=jnp.float32).astype(jnp.bfloat16)
    return mixed_out.reshape(N_BLK, TOK_DEV, D)
```

```python
import functools

import jax
import jax.numpy as jnp
from jax import lax
from jax.experimental import pallas as pl
from jax.experimental.pallas import tpu as pltpu
from jax.sharding import PartitionSpec as P

D = 1024
H = 16
HD = 64
BLK = 128
KSEL = 16
LSEL = 6
SB = 16
REACH = 8
SUMB = 4
MESH = pl.DeviceIdType.MESH
F32 = jnp.float32
BF16 = jnp.bfloat16


def kernel(
    n_head, n_blk, tok_ref, w_hbm, wo_hbm, pat_ref, out_ref,
    w_v, wo_v, kvs, qs, win, summ, q_v, m_v, l_v, acc_v, attn, ost,
    w_sem, wo_sem, kv_send, kv_recv, q_send, q_recv,
    up_send, up_recv, dn_send, dn_recv, sib_send, sib_recv,
    halo_send, halo_recv, loc_sem, out_send, out_recv,
):
    g = lax.axis_index("head")
    b = lax.axis_index("blk")
    pair = 2 * HD
    half = REACH

    def blk_at(shift):
        return lax.rem(b + n_blk + shift, n_blk)

    sibling = b + 1 - 2 * lax.rem(b, 2)

    def w_copy(k):
        dest = lax.rem(g + k, n_head)
        col = pl.multiple_of(dest * (3 * pair), pair)
        return pltpu.make_async_copy(w_hbm.at[:, pl.ds(col, 3 * pair)], w_v.at[k], w_sem.at[k])

    for k in range(n_head):
        w_copy((k + 1) % n_head).start()
    wo_copy = pltpu.make_async_copy(wo_hbm, wo_v, wo_sem)
    wo_copy.start()

    barrier = pltpu.get_barrier_semaphore()
    for k in range(1, n_head):
        pl.semaphore_signal(
            barrier, inc=1, device_id={"head": lax.rem(g + k, n_head)}, device_id_type=MESH
        )
    for shift in (-2, -1, 1, 2):
        pl.semaphore_signal(
            barrier, inc=1, device_id={"blk": blk_at(shift)}, device_id_type=MESH
        )
    pl.semaphore_wait(barrier, n_head - 1 + 4)

    low = lax.broadcasted_iota(jnp.int32, (1, pair), 1) < HD

    def remote(src, dst, send, recv, **where):
        return pltpu.make_async_remote_copy(
            src_ref=src, dst_ref=dst, send_sem=send, recv_sem=recv,
            device_id=where, device_id_type=MESH,
        )

    def own_win(h):
        return win.at[pl.ds(half + 2 * h, 2)]

    def own_sum(h):
        return summ.at[pl.ds(SUMB * b + 2 * (h - 6), 2)]

    def project(k):
        w_copy(k).wait()
        full = jnp.dot(tok_ref[...], w_v[k], preferred_element_type=F32)
        t0, t1, t2 = full[:, :pair], full[:, pair : 2 * pair], full[:, 2 * pair :]
        queries = pltpu.roll(jnp.where(low, t0, t1), HD, 1).astype(BF16) * BF16(HD**-0.5)
        keys = jnp.where(low, t2, t0).astype(BF16)
        values = jnp.where(low, t1, t2).astype(BF16)
        kvs[k, :, :, :pair] = keys.reshape(2, BLK, pair)
        kvs[k, :, :, pair:] = values.reshape(2, BLK, pair)
        qs[k] = queries.reshape(2, BLK, pair)

    def kv_to(k, dst):
        dest = lax.rem(g + k, n_head)
        return remote(kvs.at[k], dst, kv_send.at[k], kv_recv.at[g], head=dest)

    def q_to(k):
        dest = lax.rem(g + k, n_head)
        return remote(qs.at[k], q_v.at[pl.ds(2 * g, 2)], q_send.at[k], q_recv.at[g], head=dest)

    def first(k, carry):
        project(k)

        @pl.when(g < 6)
        def _():
            kv_to(k, own_win(g)).start()

        @pl.when(g >= 6)
        def _():
            kv_to(k, own_sum(g)).start()

        return carry

    lax.fori_loop(1, n_head, first, 0)
    project(0)

    @pl.when(g < 6)
    def _():
        pltpu.make_async_copy(kvs.at[0], own_win(g), kv_recv.at[g]).start()

    @pl.when(g >= 6)
    def _():
        pltpu.make_async_copy(kvs.at[0], own_sum(g), kv_recv.at[g]).start()

    for k in range(1, n_head):
        q_to(k).start()
    pltpu.make_async_copy(qs.at[0], q_v.at[pl.ds(2 * g, 2)], q_recv.at[g]).start()

    def arrived(ref, sem):
        pltpu.make_async_copy(ref, ref, sem).wait()

    def slot(source, part):
        return summ.at[SUMB * source + part]

    def up_copy(n):
        source = blk_at(-2 * (n // SUMB))
        ref = slot(source, lax.rem(n, SUMB))
        return remote(ref, ref, up_send.at[n], up_recv.at[n], blk=blk_at(2))

    def dn_copy(n):
        source = blk_at(2 * (n // SUMB))
        ref = slot(source, lax.rem(n, SUMB))
        return remote(ref, ref, dn_send.at[n], dn_recv.at[n], blk=blk_at(-2))

    def sib_copy(m, source, part):
        ref = slot(source, part)
        return remote(ref, ref, sib_send.at[m], sib_recv.at[m], blk=sibling)

    def halo_copy(h, src):
        if h < 4:
            return remote(
                src, win.at[pl.ds(3 * half + 2 * h, 2)], halo_send.at[h], halo_recv.at[h],
                blk=blk_at(-1),
            )
        return remote(
            src, win.at[pl.ds(2 * h - half, 2)], halo_send.at[h], halo_recv.at[h], blk=blk_at(1)
        )

    for h in (6, 7):
        arrived(own_sum(h), kv_recv.at[h])
        for part in (2 * (h - 6), 2 * (h - 6) + 1):
            up_copy(part).start()
            dn_copy(part).start()
            sib_copy(part, b, part).start()
        halo_copy(h, own_sum(h)).start()
        pltpu.make_async_copy(own_sum(h), own_win(h), loc_sem.at[h - 6]).start()
    for h in range(6):
        arrived(own_win(h), kv_recv.at[h])
        halo_copy(h, own_win(h)).start()

    n_up = SUMB * (n_blk // 4)
    n_dn = SUMB * (n_blk // 4 - 1)

    def relay(n):
        step, part = n // SUMB + 1, lax.rem(n, SUMB)
        source = blk_at(-2 * step)
        arrived(slot(source, part), up_recv.at[n])

        @pl.when(n < n_up - SUMB)
        def _():
            up_copy(n + SUMB).start()

        sib_copy(SUMB + n, source, part).start()

        @pl.when(n < n_dn)
        def _():
            source = blk_at(2 * step)
            arrived(slot(source, part), dn_recv.at[n])

            @pl.when(n < n_dn - SUMB)
            def _():
                dn_copy(n + SUMB).start()

            sib_copy(SUMB + n_up + n, source, part).start()

    n_pairs = n_head

    def relays(n, carry):
        relay(n)
        return carry

    lax.fori_loop(0, n_up - n_pairs, relays, 0)

    for h in range(n_head):
        arrived(q_v.at[pl.ds(2 * h, 2)], q_recv.at[h])
        if h < 4:
            arrived(win.at[pl.ds(3 * half + 2 * h, 2)], halo_recv.at[h])
        else:
            arrived(win.at[pl.ds(2 * h - half, 2)], halo_recv.at[h])
    for h in (6, 7):
        arrived(own_win(h), loc_sem.at[h - 6])

    def masked_queries(i):
        block = q_v[i]
        zero = jnp.zeros_like(block)
        return jnp.concatenate([jnp.where(low, zero, block), jnp.where(low, block, zero)], axis=0)

    def scores_of(queries, ref, places):
        keys = jnp.concatenate([ref[p, :, :pair] for p in places], axis=0)
        return lax.dot_general(
            queries, keys, (((1,), (1,)), ((), ())), preferred_element_type=F32
        )

    def mixed(weights, ref, places):
        values = jnp.concatenate([ref[p, :, pair:] for p in places], axis=0)
        return jnp.dot(weights.astype(BF16), values, preferred_element_type=F32)

    def window_block(i):
        places = [
            jnp.clip(pat_ref[i, j] - (SB * b - half), 0, SB + 2 * half - 1) for j in range(LSEL)
        ]
        scores = scores_of(masked_queries(i), win, places)
        top = jnp.max(scores, axis=1, keepdims=True)
        raised = jnp.exp(scores - top)
        total = jnp.sum(raised, axis=1, keepdims=True)
        acc_v[i] = mixed(raised, win, places)
        m_v[i] = jnp.broadcast_to(top, (2 * BLK, pair))
        l_v[i] = jnp.broadcast_to(total, (2 * BLK, pair))

    def summary_block(i):
        places = []
        for j in range(LSEL, KSEL):
            block = pat_ref[i, j]
            within = jnp.maximum(lax.rem(block, SB) - (SB - SUMB), 0)
            places.append((block // SB) * SUMB + within)
        scores = scores_of(masked_queries(i), summ, places)
        before = m_v[i]
        top = jnp.maximum(jnp.max(scores, axis=1, keepdims=True), before)
        shrink = jnp.exp(before - top)
        raised = jnp.exp(scores - top[:, :1])
        total = jnp.sum(raised, axis=1, keepdims=True) + l_v[i] * shrink
        product = (mixed(raised, summ, places) + acc_v[i] * shrink) / total
        return jnp.where(low, product[:BLK], product[BLK:]).astype(BF16)

    def window_pair(t, carry):
        window_block(2 * t)
        window_block(2 * t + 1)
        relay(n_up - n_pairs + t)
        return carry

    lax.fori_loop(0, n_pairs, window_pair, 0)

    other = sibling
    for m in range(SUMB):
        arrived(slot(other, m), sib_recv.at[m])

    def others(n, carry):
        step, part = n // SUMB + 1, lax.rem(n, SUMB)
        arrived(slot(lax.rem(other + n_blk - 2 * step, n_blk), part), sib_recv.at[SUMB + n])

        @pl.when(n < n_dn)
        def _():
            arrived(slot(lax.rem(other + 2 * step, n_blk), part), sib_recv.at[SUMB + n_up + n])

        return carry

    lax.fori_loop(0, n_up, others, 0)

    columns = pl.ds(pl.multiple_of(g * pair, pair), pair)

    def out_to(t):
        dest = lax.rem(g + 1 + t, n_head)
        return remote(ost.at[t], attn.at[:, columns], out_send.at[t], out_recv.at[g], head=dest)

    def summary_pair(t, carry):
        dest = lax.rem(g + 1 + t, n_head)
        ost[t, :BLK] = summary_block(2 * dest)
        ost[t, BLK:] = summary_block(2 * dest + 1)

        @pl.when(t < n_head - 1)
        def _():
            out_to(t).start()

        return carry

    lax.fori_loop(0, n_pairs, summary_pair, 0)
    pltpu.make_async_copy(ost.at[n_head - 1], attn.at[:, columns], out_recv.at[g]).start()

    wo_copy.wait()
    for h in range(n_head):
        arrived(attn.at[:, pl.ds(h * pair, pair)], out_recv.at[h])
    out_ref[...] = jnp.dot(attn[...], wo_v[...], preferred_element_type=F32).astype(BF16)

    for k in range(1, n_head):
        kv_to(k, own_win(0)).wait_send()
        q_to(k).wait_send()
        out_to(k - 1).wait_send()
    for h in range(n_head):
        halo_copy(h, own_win(h)).wait_send()

    def sent(n, carry):
        up_copy(n).wait_send()
        sib_copy(n, b, 0).wait_send()
        sib_copy(n_up + n, b, 0).wait_send()

        @pl.when(n < n_dn)
        def _():
            dn_copy(n).wait_send()

        return carry

    lax.fori_loop(0, n_up, sent, 0)


def on_device(n_head, n_blk, tokens, proj_weight, out_weight, pattern):
    rows = tokens.shape[1]
    pair = 2 * HD
    n_query = pattern.shape[0]
    n_up = SUMB * (n_blk // 4)
    n_dn = n_up - SUMB
    n_sib = SUMB * (n_blk // 2)
    dma = pltpu.SemaphoreType.DMA
    out = pl.pallas_call(
        functools.partial(kernel, n_head, n_blk),
        out_shape=jax.ShapeDtypeStruct((rows, D), BF16),
        in_specs=[
            pl.BlockSpec(memory_space=pltpu.VMEM),
            pl.BlockSpec(memory_space=pl.ANY),
            pl.BlockSpec(memory_space=pl.ANY),
            pl.BlockSpec(memory_space=pltpu.SMEM),
        ],
        out_specs=pl.BlockSpec(memory_space=pltpu.VMEM),
        scratch_shapes=[
            pltpu.VMEM((n_head, D, 3 * pair), BF16),
            pltpu.VMEM((D, D), BF16),
            pltpu.VMEM((n_head, 2, BLK, 2 * pair), BF16),
            pltpu.VMEM((n_head, 2, BLK, pair), BF16),
            pltpu.VMEM((SB + 2 * REACH, BLK, 2 * pair), BF16),
            pltpu.VMEM((SUMB * n_blk, BLK, 2 * pair), BF16),
            pltpu.VMEM((n_query, BLK, pair), BF16),
            pltpu.VMEM((n_query, 2 * BLK, pair), F32),
            pltpu.VMEM((n_query, 2 * BLK, pair), F32),
            pltpu.VMEM((n_query, 2 * BLK, pair), F32),
            pltpu.VMEM((rows, D), BF16),
            pltpu.VMEM((n_head, rows, pair), BF16),
            dma((n_head,)),
            dma,
            dma((n_head,)),
            dma((n_head,)),
            dma((n_head,)),
            dma((n_head,)),
            dma((n_up,)),
            dma((n_up,)),
            dma((n_dn,)),
            dma((n_dn,)),
            dma((n_sib,)),
            dma((n_sib,)),
            dma((n_head,)),
            dma((n_head,)),
            dma((2,)),
            dma((n_head,)),
            dma((n_head,)),
        ],
        compiler_params=pltpu.CompilerParams(
            collective_id=0, has_side_effects=True, vmem_limit_bytes=48 * 1024 * 1024
        ),
    )(tokens[0], proj_weight, out_weight, pattern)
    return out.reshape(1, rows, D)


def solution(mesh):
    return jax.shard_map(
        functools.partial(on_device, mesh.shape["head"], mesh.shape["blk"]),
        mesh=mesh,
        in_specs=(P(("batch", "blk"), "head", None), P(), P(), P(("batch", "blk"), None)),
        out_specs=P(("batch", "blk"), "head", None),
        check_vma=False,
    )
```

```python
import functools

import jax
import jax.numpy as jnp
from jax import lax
from jax.experimental import pallas as pl
from jax.experimental.pallas import tpu as pltpu
from jax.sharding import PartitionSpec as P

D = 1024
H = 16
HD = 64
BLK = 128
KSEL = 16
LSEL = 6
SSEL = 10
SB = 16
REACH = 8
SUMB = 4
MESH = pl.DeviceIdType.MESH
F32 = jnp.float32
BF16 = jnp.bfloat16
PAIR = 2 * HD
FIRST_SUM = (SB - SUMB) // 2


def kernel(
    n_head, n_blk, tok_hbm, w_hbm, wo_hbm, pat_hbm, out_ref,
    tok_v, w_v, wo_v, pat_ref, ks, vs, qs, win_k, win_v, sum_k, sum_v,
    q_v, ml_v, p_v, a_v, c_v, attn, ost,
    in_sem, w_sem, k_send, k_recv, v_send, v_recv, q_send, q_recv,
    up_send, up_recv, dn_send, dn_recv, sib_send, sib_recv,
    halo_send, halo_recv, loc_sem, out_send, out_recv,
):
    g = lax.axis_index("head")
    b = lax.axis_index("blk")
    core = lax.rem(b, 2)
    sibling = b + 1 - 2 * core
    half = REACH
    chunks = SUMB // 2
    summary_owner = g >= FIRST_SUM
    ks_kinds = (sum_k, sum_v)
    steps = n_blk // 4
    n_up = (chunks * steps, chunks * steps - 1)
    n_dn = (chunks * (steps - 1), chunks * (steps - 1) + 1)

    def shifted(position, shift):
        return lax.rem(position + n_blk + shift, n_blk)

    def w_copy(k):
        dest = lax.rem(g + k, n_head)
        col = pl.multiple_of(dest * (3 * PAIR), PAIR)
        return pltpu.make_async_copy(w_hbm.at[:, pl.ds(col, 3 * PAIR)], w_v.at[k], w_sem.at[k])

    tok_copy = pltpu.make_async_copy(tok_hbm, tok_v, in_sem.at[0])
    wo_copy = pltpu.make_async_copy(wo_hbm, wo_v, in_sem.at[1])
    pat_copy = pltpu.make_async_copy(pat_hbm, pat_ref, in_sem.at[2])
    tok_copy.start()
    for k in range(n_head):
        w_copy((k + 1) % n_head).start()
    pat_copy.start()
    wo_copy.start()

    barrier = pltpu.get_barrier_semaphore()
    for k in range(1, n_head):
        pl.semaphore_signal(
            barrier, inc=1, device_id={"head": lax.rem(g + k, n_head)}, device_id_type=MESH
        )
    for shift in (-2, -1, 1, 2):
        pl.semaphore_signal(
            barrier, inc=1, device_id={"blk": shifted(b, shift)}, device_id_type=MESH
        )

    low = lax.broadcasted_iota(jnp.int32, (1, PAIR), 1) < HD

    def remote(src, dst, send, recv, **where):
        return pltpu.make_async_remote_copy(
            src_ref=src, dst_ref=dst, send_sem=send, recv_sem=recv,
            device_id=where, device_id_type=MESH,
        )

    def arrived(ref, sem):
        pltpu.make_async_copy(ref, ref, sem).wait()

    def own_win(ref, h):
        return ref.at[pl.ds(half + 2 * h, 2)]

    def own_sum(ref, h):
        return ref.at[pl.ds(SUMB * b + 2 * (h - FIRST_SUM), 2)]

    def project(k, carry):
        w_copy(k).wait()
        full = jnp.dot(tok_v[...], w_v[k], preferred_element_type=F32)
        t0, t1, t2 = full[:, :PAIR], full[:, PAIR : 2 * PAIR], full[:, 2 * PAIR :]
        queries = pltpu.roll(jnp.where(low, t0, t1), HD, 1).astype(BF16) * BF16(HD**-0.5)
        ks[k] = jnp.where(low, t2, t0).astype(BF16).reshape(2, BLK, PAIR)
        vs[k] = jnp.where(low, t1, t2).astype(BF16).reshape(2, BLK, PAIR)
        qs[k] = queries.reshape(2, BLK, PAIR)
        return carry

    tok_copy.wait()
    lax.fori_loop(1, n_head, project, 0)
    project(0, 0)
    pl.semaphore_wait(barrier, n_head - 1 + 4)

    def exchange(stage, send, recv, k, dst):
        return remote(stage.at[k], dst, send.at[k], recv.at[g], head=lax.rem(g + k, n_head))

    def send_all(stage, send, recv, dst):
        for k in range(1, n_head):
            exchange(stage, send, recv, k, dst).start()
        pltpu.make_async_copy(stage.at[0], dst, recv.at[g]).start()

    own_q = q_v.at[pl.ds(2 * g, 2)]

    @pl.when(summary_owner)
    def _():
        send_all(ks, k_send, k_recv, own_sum(sum_k, g))

    send_all(qs, q_send, q_recv, own_q)

    @pl.when(summary_owner)
    def _():
        send_all(vs, v_send, v_recv, own_sum(sum_v, g))

    def piece(kind, source, part):
        return ks_kinds[kind].at[pl.ds(SUMB * source + 2 * part, 2)]

    def dn_part(kind, n):
        part = lax.rem(n, chunks)
        return part if kind == 0 else chunks - 1 - part

    def up_copy(kind, n):
        ref = piece(kind, shifted(b, -2 * (n // chunks)), lax.rem(n, chunks))
        return remote(
            ref, ref, up_send.at[kind, n], up_recv.at[kind, n], blk=shifted(b, 2)
        )

    def dn_copy(kind, n):
        ref = piece(kind, shifted(b, 2 * (n // chunks)), dn_part(kind, n))
        return remote(
            ref, ref, dn_send.at[kind, n], dn_recv.at[kind, n], blk=shifted(b, -2)
        )

    def sib_copy(kind, m, ref):
        return remote(ref, ref, sib_send.at[kind, m], sib_recv.at[kind, m], blk=sibling)

    def start_own(kind):
        for part in range(chunks):
            ref = piece(kind, b, part)
            h = FIRST_SUM + part
            arrived(ref, (k_recv, v_recv)[kind].at[h])
            up_copy(kind, part).start()
            dn_copy(kind, part if kind == 0 else chunks - 1 - part).start()
            sib_copy(kind, part, ref).start()
            pltpu.make_async_copy(
                ref, own_win((win_k, win_v)[kind], h), loc_sem.at[kind, part]
            ).start()

    def relay(kind, n):
        ref = piece(kind, shifted(b, -2 * (n // chunks + 1)), lax.rem(n, chunks))
        arrived(ref, up_recv.at[kind, n])

        @pl.when(n < n_up[kind] - chunks)
        def _():
            up_copy(kind, n + chunks).start()

        sib_copy(kind, chunks + n, ref).start()

        @pl.when(n < n_dn[kind])
        def _():
            back = piece(kind, shifted(b, 2 * (n // chunks + 1)), dn_part(kind, n))
            arrived(back, dn_recv.at[kind, n])

            @pl.when(n < n_dn[kind] - chunks)
            def _():
                dn_copy(kind, n + chunks).start()

            sib_copy(kind, chunks + n_up[kind] + n, back).start()

    start_own(0)

    @pl.when(jnp.logical_not(summary_owner))
    def _():
        send_all(ks, k_send, k_recv, own_win(win_k, g))
        send_all(vs, v_send, v_recv, own_win(win_v, g))

    def relays(n, carry):
        relay(0, n)
        return carry

    lax.fori_loop(0, n_up[0] - chunks, relays, 0)
    start_own(1)
    lax.fori_loop(n_up[0] - chunks, n_up[0], relays, 0)

    early = chunks * (1 - core)

    def other_arrived(kind, m):
        s = sibling
        if kind == 0:
            down_part = lambda n: lax.rem(n, chunks)
        else:
            down_part = lambda n: chunks - 1 - lax.rem(n, chunks)

        @pl.when(m < chunks)
        def _():
            arrived(piece(kind, s, m), sib_recv.at[kind, m])

        n = m - chunks

        @pl.when(jnp.logical_and(n >= 0, n < n_up[kind]))
        def _():
            arrived(
                piece(kind, shifted(s, -2 * (n // chunks + 1)), lax.rem(n, chunks)),
                sib_recv.at[kind, m],
            )

        n2 = n - n_up[kind]

        @pl.when(n2 >= 0)
        def _():
            arrived(
                piece(kind, shifted(s, 2 * (n2 // chunks + 1)), down_part(n2)),
                sib_recv.at[kind, m],
            )

    def copy_below(kind):
        for part in range(chunks):
            other_arrived(kind, early + part)
            pltpu.make_async_copy(
                piece(kind, shifted(b, -1), part),
                (win_k, win_v)[kind].at[pl.ds(SUMB + 2 * part, 2)],
                loc_sem.at[kind, chunks + part],
            ).start()

    def others(kind):
        def body(m, carry):
            @pl.when(jnp.logical_or(m < early, m >= early + chunks))
            def _():
                other_arrived(kind, m)

            return carry

        lax.fori_loop(0, chunks * n_blk // 2, body, 0)

    def halo_place(ref, h):
        start = 3 * half + 2 * h if 2 * h < half else 2 * h - half
        return ref.at[pl.ds(start, 2)]

    def halo_copy(kind, h):
        ref = (win_k, win_v)[kind]
        shift = -1 if 2 * h < half else 1
        return remote(
            own_win(ref, h), halo_place(ref, h), halo_send.at[kind, h], halo_recv.at[kind, h],
            blk=shifted(b, shift),
        )

    copy_below(0)
    others(0)
    for h in range(n_head):
        arrived(q_v.at[pl.ds(2 * h, 2)], q_recv.at[h])
    pat_copy.wait()

    def masked_queries(i):
        block = q_v[i]
        zero = jnp.zeros_like(block)
        return jnp.concatenate([jnp.where(low, zero, block), jnp.where(low, block, zero)], axis=0)

    def scores_of(queries, ref, places):
        keys = jnp.concatenate([ref[p] for p in places], axis=0)
        return lax.dot_general(
            queries, keys, (((1,), (1,)), ((), ())), preferred_element_type=F32
        )

    def mixed(weights, ref, places):
        values = jnp.concatenate([ref[p] for p in places], axis=0)
        return jnp.dot(weights, values, preferred_element_type=F32)

    def by_head(rows):
        return jnp.where(low, rows[:BLK], rows[BLK:])

    def summary_places(i):
        places = []
        for j in range(LSEL, KSEL):
            block = pat_ref[i, j]
            within = jnp.maximum(lax.rem(block, SB) - (SB - SUMB), 0)
            places.append((block // SB) * SUMB + within)
        return places

    def summary_weights(i):
        scores = scores_of(masked_queries(i), sum_k, summary_places(i))
        top = jnp.max(scores, axis=1, keepdims=True)
        raised = jnp.exp(scores - top)
        p_v[i] = raised.astype(BF16)
        total = jnp.sum(raised, axis=1, keepdims=True)
        ml_v[i] = jnp.where(low, top, total)

    def window_block(i):
        places = [
            jnp.clip(pat_ref[i, j] - (SB * b - half), 0, SB + 2 * half - 1) for j in range(LSEL)
        ]
        scores = scores_of(masked_queries(i), win_k, places)
        kept = ml_v[i]
        far_top, far_total = kept[:, :1], kept[:, HD : HD + 1]
        top = jnp.maximum(jnp.max(scores, axis=1, keepdims=True), far_top)
        raised = jnp.exp(scores - top)
        shrink = jnp.exp(far_top - top)
        inverse = 1.0 / (jnp.sum(raised, axis=1, keepdims=True) + far_total * shrink)
        a_v[i] = by_head(mixed(raised.astype(BF16), win_v, places) * inverse)
        c_v[i] = by_head(jnp.broadcast_to(shrink * inverse, (2 * BLK, PAIR)))

    def finish_block(i):
        product = mixed(p_v[i], sum_v, summary_places(i))
        return (a_v[i] + c_v[i] * by_head(product)).astype(BF16)

    def weights_pair(t, carry):
        summary_weights(2 * t)
        summary_weights(2 * t + 1)

        @pl.when(t < n_up[1])
        def _():
            relay(1, t)

        @pl.when(t == 2)
        def _():
            for h in range(FIRST_SUM):
                for kind in range(2):
                    arrived(own_win((win_k, win_v)[kind], h), (k_recv, v_recv)[kind].at[h])
                    halo_copy(kind, h).start()

        return carry

    lax.fori_loop(0, n_head, weights_pair, 0)

    copy_below(1)
    for kind in range(2):
        ref = (win_k, win_v)[kind]
        for h in range(FIRST_SUM):
            arrived(halo_place(ref, h), halo_recv.at[kind, h])
        for part in range(chunks):
            arrived(own_win(ref, FIRST_SUM + part), loc_sem.at[kind, part])
            arrived(ref.at[pl.ds(SUMB + 2 * part, 2)], loc_sem.at[kind, chunks + part])

    def window_pair(t, carry):
        window_block(2 * t)
        window_block(2 * t + 1)
        return carry

    lax.fori_loop(0, n_head, window_pair, 0)
    others(1)

    columns = pl.ds(pl.multiple_of(g * PAIR, PAIR), PAIR)

    def out_to(t):
        dest = lax.rem(g + 1 + t, n_head)
        return remote(ost.at[t], attn.at[:, columns], out_send.at[t], out_recv.at[g], head=dest)

    def finish_pair(t, carry):
        dest = lax.rem(g + 1 + t, n_head)
        ost[t, :BLK] = finish_block(2 * dest)
        ost[t, BLK:] = finish_block(2 * dest + 1)

        @pl.when(t < n_head - 1)
        def _():
            out_to(t).start()

        return carry

    lax.fori_loop(0, n_head, finish_pair, 0)
    pltpu.make_async_copy(ost.at[n_head - 1], attn.at[:, columns], out_recv.at[g]).start()

    wo_copy.wait()
    for h in range(n_head):
        arrived(attn.at[:, pl.ds(h * PAIR, PAIR)], out_recv.at[h])
    out_ref[...] = jnp.dot(attn[...], wo_v[...], preferred_element_type=F32).astype(BF16)

    for k in range(1, n_head):
        exchange(ks, k_send, k_recv, k, own_q).wait_send()
        exchange(vs, v_send, v_recv, k, own_q).wait_send()
        exchange(qs, q_send, q_recv, k, own_q).wait_send()
        out_to(k - 1).wait_send()
    for kind in range(2):
        for h in range(FIRST_SUM):
            halo_copy(kind, h).wait_send()

        def sent(m, carry, kind=kind):
            sib_copy(kind, m, piece(kind, b, 0)).wait_send()

            @pl.when(m < n_up[kind])
            def _():
                up_copy(kind, m).wait_send()

            @pl.when(m < n_dn[kind])
            def _():
                dn_copy(kind, m).wait_send()

            return carry

        lax.fori_loop(0, chunks * n_blk // 2, sent, 0)


def on_device(n_head, n_blk, tokens, proj_weight, out_weight, pattern):
    rows = tokens.shape[1]
    n_query = pattern.shape[0]
    n_hop = SUMB * (n_blk // 8)
    n_sib = SUMB * (n_blk // 4)
    dma = pltpu.SemaphoreType.DMA
    blocks = lambda *lead: pltpu.VMEM((*lead, BLK, PAIR), BF16)
    out = pl.pallas_call(
        functools.partial(kernel, n_head, n_blk),
        out_shape=jax.ShapeDtypeStruct((rows, D), BF16),
        in_specs=[pl.BlockSpec(memory_space=pl.ANY)] * 4,
        out_specs=pl.BlockSpec(memory_space=pltpu.VMEM),
        scratch_shapes=[
            pltpu.VMEM((rows, D), BF16),
            pltpu.VMEM((n_head, D, 3 * PAIR), BF16),
            pltpu.VMEM((D, D), BF16),
            pltpu.SMEM((n_query, KSEL), jnp.int32),
            blocks(n_head, 2),
            blocks(n_head, 2),
            blocks(n_head, 2),
            blocks(SB + 2 * REACH),
            blocks(SB + 2 * REACH),
            blocks(SUMB * n_blk),
            blocks(SUMB * n_blk),
            blocks(n_query),
            pltpu.VMEM((n_query, 2 * BLK, PAIR), F32),
            pltpu.VMEM((n_query, 2 * BLK, SSEL * BLK), BF16),
            pltpu.VMEM((n_query, BLK, PAIR), F32),
            pltpu.VMEM((n_query, BLK, PAIR), F32),
            pltpu.VMEM((rows, D), BF16),
            pltpu.VMEM((n_head, rows, PAIR), BF16),
            dma((3,)),
            dma((n_head,)),
            dma((n_head,)),
            dma((n_head,)),
            dma((n_head,)),
            dma((n_head,)),
            dma((n_head,)),
            dma((n_head,)),
            dma((2, n_hop)),
            dma((2, n_hop)),
            dma((2, n_hop)),
            dma((2, n_hop)),
            dma((2, n_sib)),
            dma((2, n_sib)),
            dma((2, FIRST_SUM)),
            dma((2, FIRST_SUM)),
            dma((2, SUMB)),
            dma((n_head,)),
            dma((n_head,)),
        ],
        compiler_params=pltpu.CompilerParams(
            collective_id=0, has_side_effects=True, vmem_limit_bytes=56 * 1024 * 1024
        ),
    )(tokens[0], proj_weight, out_weight, pattern)
    return out.reshape(1, rows, D)


def solution(mesh):
    return jax.shard_map(
        functools.partial(on_device, mesh.shape["head"], mesh.shape["blk"]),
        mesh=mesh,
        in_specs=(P(("batch", "blk"), "head", None), P(), P(), P(("batch", "blk"), None)),
        out_specs=P(("batch", "blk"), "head", None),
        check_vma=False,
    )
```

```python
import functools

import jax
import jax.numpy as jnp
from jax import lax
from jax.experimental import pallas as pl
from jax.experimental.pallas import tpu as pltpu
from jax.sharding import PartitionSpec as P

D = 1024
H = 16
HD = 64
BLK = 128
KSEL = 16
LSEL = 6
SSEL = 10
SB = 16
REACH = 8
SUMB = 4
MESH = pl.DeviceIdType.MESH
F32 = jnp.float32
BF16 = jnp.bfloat16
PAIR = 2 * HD
FIRST_SUM = (SB - SUMB) // 2


def kernel(
    n_head, n_blk, tok_hbm, w_hbm, wo_hbm, pat_hbm, out_ref,
    tok_v, w_v, wo_v, pat_ref, ks, vs, qs, win_k, win_v, sum_k, sum_v,
    q_v, m_v, p_v, near_v, near_m, s_a, s_b, attn, ost,
    in_sem, w_sem, k_send, k_recv, v_send, v_recv, q_send, q_recv,
    up_send, up_recv, dn_send, dn_recv, sib_send, sib_recv,
    halo_send, halo_recv, loc_sem, out_send, out_recv,
):
    g = lax.axis_index("head")
    b = lax.axis_index("blk")
    core = lax.rem(b, 2)
    sibling = b + 1 - 2 * core
    half = REACH
    chunks = SUMB // 2
    summary_owner = g >= FIRST_SUM
    ks_kinds = (sum_k, sum_v)
    steps = n_blk // 4
    n_up = (chunks * steps, chunks * steps - 1)
    n_dn = (chunks * (steps - 1), chunks * (steps - 1) + 1)

    def shifted(position, shift):
        return lax.rem(position + n_blk + shift, n_blk)

    def w_copy(k):
        dest = lax.rem(g + k, n_head)
        col = pl.multiple_of(dest * (3 * PAIR), PAIR)
        return pltpu.make_async_copy(w_hbm.at[:, pl.ds(col, 3 * PAIR)], w_v.at[k], w_sem.at[k])

    tok_copy = pltpu.make_async_copy(tok_hbm, tok_v, in_sem.at[0])
    wo_copy = pltpu.make_async_copy(wo_hbm, wo_v, in_sem.at[1])
    pat_copy = pltpu.make_async_copy(pat_hbm, pat_ref, in_sem.at[2])
    tok_copy.start()
    for k in range(n_head):
        w_copy((k + 1) % n_head).start()
    pat_copy.start()
    wo_copy.start()

    barrier = pltpu.get_barrier_semaphore()
    for k in range(1, n_head):
        pl.semaphore_signal(
            barrier, inc=1, device_id={"head": lax.rem(g + k, n_head)}, device_id_type=MESH
        )
    for shift in (-2, -1, 1, 2):
        pl.semaphore_signal(
            barrier, inc=1, device_id={"blk": shifted(b, shift)}, device_id_type=MESH
        )

    low = lax.broadcasted_iota(jnp.int32, (1, PAIR), 1) < HD

    def remote(src, dst, send, recv, **where):
        return pltpu.make_async_remote_copy(
            src_ref=src, dst_ref=dst, send_sem=send, recv_sem=recv,
            device_id=where, device_id_type=MESH,
        )

    def arrived(ref, sem):
        pltpu.make_async_copy(ref, ref, sem).wait()

    def own_win(ref, h):
        return ref.at[pl.ds(half + 2 * h, 2)]

    def own_sum(ref, h):
        return ref.at[pl.ds(SUMB * b + 2 * (h - FIRST_SUM), 2)]

    def project(k, carry):
        w_copy(k).wait()
        full = jnp.dot(tok_v[...], w_v[k], preferred_element_type=F32)
        t0, t1, t2 = full[:, :PAIR], full[:, PAIR : 2 * PAIR], full[:, 2 * PAIR :]
        queries = pltpu.roll(jnp.where(low, t0, t1), HD, 1).astype(BF16) * BF16(HD**-0.5)
        ks[k] = jnp.where(low, t2, t0).astype(BF16).reshape(2, BLK, PAIR)
        values = jnp.where(low, t1, t2)
        for half_block in range(2):
            vs[k, half_block] = values[half_block * BLK : (half_block + 1) * BLK].T.astype(BF16)
        qs[k] = queries.reshape(2, BLK, PAIR)
        return carry

    def exchange(stage, send, recv, k, dst):
        return remote(stage.at[k], dst, send.at[k], recv.at[g], head=lax.rem(g + k, n_head))

    own_q = q_v.at[pl.ds(2 * g, 2)]

    def send_all(stage, send, recv, dst):
        for k in range(1, n_head):
            exchange(stage, send, recv, k, dst).start()
        pltpu.make_async_copy(stage.at[0], dst, recv.at[g]).start()

    def send_far_keys(k):
        @pl.when(summary_owner)
        def _():
            exchange(ks, k_send, k_recv, k, own_sum(sum_k, g)).start()

    def project_and_send(k, carry):
        project(k, carry)
        send_far_keys(k)
        return carry

    tok_copy.wait()
    early_groups = 3
    lax.fori_loop(1, 1 + early_groups, project, 0)
    pl.semaphore_wait(barrier, n_head - 1 + 4)
    for k in range(1, 1 + early_groups):
        send_far_keys(k)
    lax.fori_loop(1 + early_groups, n_head, project_and_send, 0)
    project(0, 0)

    @pl.when(summary_owner)
    def _():
        pltpu.make_async_copy(ks.at[0], own_sum(sum_k, g), k_recv.at[g]).start()
        send_all(vs, v_send, v_recv, own_sum(sum_v, g))

    @pl.when(jnp.logical_not(summary_owner))
    def _():
        send_all(qs, q_send, q_recv, own_q)

    def piece(kind, source, part):
        return ks_kinds[kind].at[pl.ds(SUMB * source + 2 * part, 2)]

    def dn_part(kind, n):
        part = lax.rem(n, chunks)
        return part if kind == 0 else chunks - 1 - part

    def up_copy(kind, n):
        ref = piece(kind, shifted(b, -2 * (n // chunks)), lax.rem(n, chunks))
        return remote(
            ref, ref, up_send.at[kind, n], up_recv.at[kind, n], blk=shifted(b, 2)
        )

    def dn_copy(kind, n):
        ref = piece(kind, shifted(b, 2 * (n // chunks)), dn_part(kind, n))
        return remote(
            ref, ref, dn_send.at[kind, n], dn_recv.at[kind, n], blk=shifted(b, -2)
        )

    def sib_copy(kind, m, ref):
        return remote(ref, ref, sib_send.at[kind, m], sib_recv.at[kind, m], blk=sibling)

    def start_own(kind):
        for part in range(chunks):
            ref = piece(kind, b, part)
            h = FIRST_SUM + part
            arrived(ref, (k_recv, v_recv)[kind].at[h])
            up_copy(kind, part).start()
            dn_copy(kind, part if kind == 0 else chunks - 1 - part).start()
            sib_copy(kind, part, ref).start()
            pltpu.make_async_copy(
                ref, own_win((win_k, win_v)[kind], h), loc_sem.at[kind, part]
            ).start()

    def relay(kind, n):
        ref = piece(kind, shifted(b, -2 * (n // chunks + 1)), lax.rem(n, chunks))
        arrived(ref, up_recv.at[kind, n])

        @pl.when(n < n_up[kind] - chunks)
        def _():
            up_copy(kind, n + chunks).start()

        sib_copy(kind, chunks + n, ref).start()

        @pl.when(n < n_dn[kind])
        def _():
            back = piece(kind, shifted(b, 2 * (n // chunks + 1)), dn_part(kind, n))
            arrived(back, dn_recv.at[kind, n])

            @pl.when(n < n_dn[kind] - chunks)
            def _():
                dn_copy(kind, n + chunks).start()

            sib_copy(kind, chunks + n_up[kind] + n, back).start()

    start_own(0)

    @pl.when(jnp.logical_not(summary_owner))
    def _():
        send_all(ks, k_send, k_recv, own_win(win_k, g))
        send_all(vs, v_send, v_recv, own_win(win_v, g))

    for n in range(chunks):
        relay(0, n)
    start_own(1)

    @pl.when(summary_owner)
    def _():
        send_all(qs, q_send, q_recv, own_q)

    def relays(n, carry):
        relay(0, n)
        relay(1, n - chunks)
        return carry

    lax.fori_loop(chunks, 2 * chunks, relays, 0)

    early = chunks * (1 - core)

    def other_arrived(kind, m):
        s = sibling
        if kind == 0:
            down_part = lambda n: lax.rem(n, chunks)
        else:
            down_part = lambda n: chunks - 1 - lax.rem(n, chunks)

        @pl.when(m < chunks)
        def _():
            arrived(piece(kind, s, m), sib_recv.at[kind, m])

        n = m - chunks

        @pl.when(jnp.logical_and(n >= 0, n < n_up[kind]))
        def _():
            arrived(
                piece(kind, shifted(s, -2 * (n // chunks + 1)), lax.rem(n, chunks)),
                sib_recv.at[kind, m],
            )

        n2 = n - n_up[kind]

        @pl.when(n2 >= 0)
        def _():
            arrived(
                piece(kind, shifted(s, 2 * (n2 // chunks + 1)), down_part(n2)),
                sib_recv.at[kind, m],
            )

    def copy_below(kind):
        for part in range(chunks):
            other_arrived(kind, early + part)
            pltpu.make_async_copy(
                piece(kind, shifted(b, -1), part),
                (win_k, win_v)[kind].at[pl.ds(SUMB + 2 * part, 2)],
                loc_sem.at[kind, chunks + part],
            ).start()

    def others(kind):
        def body(m, carry):
            @pl.when(jnp.logical_or(m < early, m >= early + chunks))
            def _():
                other_arrived(kind, m)

            return carry

        lax.fori_loop(0, chunks * n_blk // 2, body, 0)

    def halo_place(ref, h):
        start = 3 * half + 2 * h if 2 * h < half else 2 * h - half
        return ref.at[pl.ds(start, 2)]

    def halo_copy(kind, h):
        ref = (win_k, win_v)[kind]
        shift = -1 if 2 * h < half else 1
        return remote(
            own_win(ref, h), halo_place(ref, h), halo_send.at[kind, h], halo_recv.at[kind, h],
            blk=shifted(b, shift),
        )

    for h in range(FIRST_SUM):
        for kind in range(2):
            arrived(own_win((win_k, win_v)[kind], h), (k_recv, v_recv)[kind].at[h])
            halo_copy(kind, h).start()
    lax.fori_loop(2 * chunks, n_up[0] - chunks, relays, 0)
    for kind in range(2):
        copy_below(kind)
    for h in range(n_head):
        arrived(q_v.at[pl.ds(2 * h, 2)], q_recv.at[h])
    pat_copy.wait()

    def masked_queries(i):
        block = q_v[i]
        zero = jnp.zeros_like(block)
        return jnp.concatenate([jnp.where(low, zero, block), jnp.where(low, block, zero)], axis=0)

    def scores_of(i, ref, places):
        keys = jnp.concatenate([ref[p] for p in places], axis=0)
        return lax.dot_general(
            keys, masked_queries(i), (((1,), (1,)), ((), ())), preferred_element_type=F32
        )

    ones = jnp.ones((16, BLK), BF16)

    def mixed(weights, ref, places):
        values = jnp.concatenate(
            [jnp.concatenate([ref[p], ones], axis=0) for p in places], axis=1
        )
        product = jnp.dot(values, weights, preferred_element_type=F32)
        return (
            (product[:HD, :BLK], product[HD:PAIR, BLK:]),
            product[PAIR : PAIR + 1],
        )

    def summary_places(i):
        places = []
        for j in range(LSEL, KSEL):
            block = pat_ref[i, j]
            within = jnp.maximum(lax.rem(block, SB) - (SB - SUMB), 0)
            places.append((block // SB) * SUMB + within)
        return places

    def summary_scores(i, buffer):
        scores = scores_of(i, sum_k, summary_places(i))
        buffer[...] = scores
        m_v[i] = jnp.broadcast_to(jnp.max(scores, axis=0, keepdims=True), (8, 2 * BLK))

    def summary_raise(i, buffer, top):
        p_v[i] = jnp.exp(buffer[...] - top).astype(BF16)

    def window_places(i):
        return [
            jnp.clip(pat_ref[i, j] - (SB * b - half), 0, SB + 2 * half - 1) for j in range(LSEL)
        ]

    near_rows = LSEL * BLK

    def window_scores(i, buffer):
        scores = scores_of(i, win_k, window_places(i))
        buffer[:near_rows] = scores
        near_m[i, :8] = jnp.broadcast_to(jnp.max(scores, axis=0, keepdims=True), (8, 2 * BLK))

    def window_mix(i, buffer, top):
        weights = jnp.exp(buffer[:near_rows] - top).astype(BF16)
        products, total = mixed(weights, win_v, window_places(i))
        near_v[i] = jnp.concatenate(products, axis=0)
        near_m[i, 8:] = jnp.broadcast_to(total, (8, 2 * BLK))

    def finish_block(i):
        products, far_total = mixed(p_v[i], sum_v, summary_places(i))
        far_top, near_top, near_total = m_v[i, :1], near_m[i, :1], near_m[i, 8:9]
        top = jnp.maximum(far_top, near_top)
        far, near = jnp.exp(far_top - top), jnp.exp(near_top - top)
        inverse = 1.0 / (far_total * far + near_total * near)
        far, near = far * inverse, near * inverse
        rows = []
        for which in range(2):
            lanes = slice(which * BLK, (which + 1) * BLK)
            near_part = near_v[i, which * HD : (which + 1) * HD]
            rows.append(products[which] * far[:, lanes] + near_part * near[:, lanes])
        return jnp.concatenate(rows, axis=0).T.astype(BF16)

    for kind in range(2):
        ref = (win_k, win_v)[kind]
        for h in range(FIRST_SUM):
            arrived(halo_place(ref, h), halo_recv.at[kind, h])
        for part in range(chunks):
            arrived(own_win(ref, FIRST_SUM + part), loc_sem.at[kind, part])
            arrived(ref.at[pl.ds(SUMB + 2 * part, 2)], loc_sem.at[kind, chunks + part])

    n_query = 2 * n_head

    def pipelined_pair(t, scores, use, tops):
        first, second = 2 * t, 2 * t + 1
        after = jnp.minimum(2 * t + 2, n_query - 1)
        top = tops[first, :1]
        scores(second, s_b)
        use(first, s_a, top)
        top = tops[second, :1]
        scores(after, s_a)
        use(second, s_b, top)

    window_scores(0, s_a)

    def window_pair(t, carry):
        pipelined_pair(t, window_scores, window_mix, near_m)

        @pl.when(t < chunks)
        def _():
            relay(0, n_up[0] - chunks + t)

        @pl.when(t < n_up[1] + 2 * chunks - n_up[0])
        def _():
            relay(1, n_up[0] - 2 * chunks + t)

        return carry

    lax.fori_loop(0, n_head, window_pair, 0)
    others(0)

    summary_scores(0, s_a)

    def weights_pair(t, carry):
        pipelined_pair(t, summary_scores, summary_raise, m_v)
        return carry

    lax.fori_loop(0, n_head, weights_pair, 0)
    others(1)

    columns = pl.ds(pl.multiple_of(g * PAIR, PAIR), PAIR)

    def out_to(t):
        dest = lax.rem(g + 1 + t, n_head)
        return remote(ost.at[t], attn.at[:, columns], out_send.at[t], out_recv.at[g], head=dest)

    def finish_pair(t, carry):
        dest = lax.rem(g + 1 + t, n_head)
        ost[t, :BLK] = finish_block(2 * dest)
        ost[t, BLK:] = finish_block(2 * dest + 1)

        @pl.when(t < n_head - 1)
        def _():
            out_to(t).start()

        return carry

    lax.fori_loop(0, n_head, finish_pair, 0)
    pltpu.make_async_copy(ost.at[n_head - 1], attn.at[:, columns], out_recv.at[g]).start()

    wo_copy.wait()
    for h in range(n_head):
        arrived(attn.at[:, pl.ds(h * PAIR, PAIR)], out_recv.at[h])
    out_ref[...] = jnp.dot(attn[...], wo_v[...], preferred_element_type=F32).astype(BF16)

    for k in range(1, n_head):
        exchange(ks, k_send, k_recv, k, own_q).wait_send()
        exchange(vs, v_send, v_recv, k, own_q).wait_send()
        exchange(qs, q_send, q_recv, k, own_q).wait_send()
        out_to(k - 1).wait_send()
    for kind in range(2):
        for h in range(FIRST_SUM):
            halo_copy(kind, h).wait_send()

        def sent(m, carry, kind=kind):
            sib_copy(kind, m, piece(kind, b, 0)).wait_send()

            @pl.when(m < n_up[kind])
            def _():
                up_copy(kind, m).wait_send()

            @pl.when(m < n_dn[kind])
            def _():
                dn_copy(kind, m).wait_send()

            return carry

        lax.fori_loop(0, chunks * n_blk // 2, sent, 0)


def on_device(n_head, n_blk, tokens, proj_weight, out_weight, pattern):
    rows = tokens.shape[1]
    n_query = pattern.shape[0]
    n_hop = SUMB * (n_blk // 8)
    n_sib = SUMB * (n_blk // 4)
    dma = pltpu.SemaphoreType.DMA
    blocks = lambda *lead: pltpu.VMEM((*lead, BLK, PAIR), BF16)
    out = pl.pallas_call(
        functools.partial(kernel, n_head, n_blk),
        out_shape=jax.ShapeDtypeStruct((rows, D), BF16),
        in_specs=[pl.BlockSpec(memory_space=pl.ANY)] * 4,
        out_specs=pl.BlockSpec(memory_space=pltpu.VMEM),
        scratch_shapes=[
            pltpu.VMEM((rows, D), BF16),
            pltpu.VMEM((n_head, D, 3 * PAIR), BF16),
            pltpu.VMEM((D, D), BF16),
            pltpu.SMEM((n_query, KSEL), jnp.int32),
            blocks(n_head, 2),
            blocks(n_head, 2),
            blocks(n_head, 2),
            blocks(SB + 2 * REACH),
            blocks(SB + 2 * REACH),
            blocks(SUMB * n_blk),
            blocks(SUMB * n_blk),
            blocks(n_query),
            pltpu.VMEM((n_query, 8, 2 * BLK), F32),
            pltpu.VMEM((n_query, SSEL * BLK, 2 * BLK), BF16),
            pltpu.VMEM((n_query, PAIR, BLK), F32),
            pltpu.VMEM((n_query, 16, 2 * BLK), F32),
            pltpu.VMEM((SSEL * BLK, 2 * BLK), F32),
            pltpu.VMEM((SSEL * BLK, 2 * BLK), F32),
            pltpu.VMEM((rows, D), BF16),
            pltpu.VMEM((n_head, rows, PAIR), BF16),
            dma((3,)),
            dma((n_head,)),
            dma((n_head,)),
            dma((n_head,)),
            dma((n_head,)),
            dma((n_head,)),
            dma((n_head,)),
            dma((n_head,)),
            dma((2, n_hop)),
            dma((2, n_hop)),
            dma((2, n_hop)),
            dma((2, n_hop)),
            dma((2, n_sib)),
            dma((2, n_sib)),
            dma((2, FIRST_SUM)),
            dma((2, FIRST_SUM)),
            dma((2, SUMB)),
            dma((n_head,)),
            dma((n_head,)),
        ],
        compiler_params=pltpu.CompilerParams(
            collective_id=0, has_side_effects=True, vmem_limit_bytes=53 * 1024 * 1024
        ),
    )(tokens[0], proj_weight, out_weight, pattern)
    return out.reshape(1, rows, D)


def solution(mesh):
    return jax.shard_map(
        functools.partial(on_device, mesh.shape["head"], mesh.shape["blk"]),
        mesh=mesh,
        in_specs=(P(("batch", "blk"), "head", None), P(), P(), P(("batch", "blk"), None)),
        out_specs=P(("batch", "blk"), "head", None),
        check_vma=False,
    )
```

```python
import functools

import jax
import jax.numpy as jnp
from jax import lax
from jax.experimental import pallas as pl
from jax.experimental.pallas import tpu as pltpu
from jax.sharding import PartitionSpec as P

D = 1024
H = 16
HD = 64
BLK = 128
KSEL = 16
LSEL = 6
SSEL = 10
SB = 16
REACH = 8
SUMB = 4
MESH = pl.DeviceIdType.MESH
F32 = jnp.float32
BF16 = jnp.bfloat16
PAIR = 2 * HD
FIRST_SUM = (SB - SUMB) // 2


def kernel(
    n_head, n_blk, tok_hbm, w_hbm, wo_hbm, pat_hbm, out_ref,
    tok_v, w_v, wo_v, pat_ref, ks, vs, qs, win_k, win_v, sum_k, sum_v,
    q_v, m_v, p_v, near_v, near_m, s_a, s_b, attn, ost,
    in_sem, w_sem, k_send, k_recv, v_send, v_recv, q_send, q_recv,
    up_send, up_recv, dn_send, dn_recv, sib_send, sib_recv,
    halo_send, halo_recv, loc_sem, out_send, out_recv,
):
    g = lax.axis_index("head")
    b = lax.axis_index("blk")
    core = lax.rem(b, 2)
    sibling = b + 1 - 2 * core
    half = REACH
    chunks = SUMB // 2
    summary_owner = g >= FIRST_SUM
    ks_kinds = (sum_k, sum_v)
    steps = n_blk // 4
    n_up = (chunks * steps, chunks * steps - 1)
    n_dn = (chunks * (steps - 1), chunks * (steps - 1) + 1)

    def shifted(position, shift):
        return lax.rem(position + n_blk + shift, n_blk)

    def w_copy(k):
        dest = lax.rem(g + k, n_head)
        col = pl.multiple_of(dest * (3 * PAIR), PAIR)
        return pltpu.make_async_copy(w_hbm.at[:, pl.ds(col, 3 * PAIR)], w_v.at[k], w_sem.at[k])

    tok_copy = pltpu.make_async_copy(tok_hbm, tok_v, in_sem.at[0])
    wo_copy = pltpu.make_async_copy(wo_hbm, wo_v, in_sem.at[1])
    pat_copy = pltpu.make_async_copy(pat_hbm, pat_ref, in_sem.at[2])
    tok_copy.start()
    for k in range(n_head):
        w_copy((k + 1) % n_head).start()
    pat_copy.start()
    wo_copy.start()

    barrier = pltpu.get_barrier_semaphore()
    for k in range(1, n_head):
        pl.semaphore_signal(
            barrier, inc=1, device_id={"head": lax.rem(g + k, n_head)}, device_id_type=MESH
        )
    for shift in (-2, -1, 1, 2):
        pl.semaphore_signal(
            barrier, inc=1, device_id={"blk": shifted(b, shift)}, device_id_type=MESH
        )

    low = lax.broadcasted_iota(jnp.int32, (1, PAIR), 1) < HD

    def remote(src, dst, send, recv, **where):
        return pltpu.make_async_remote_copy(
            src_ref=src, dst_ref=dst, send_sem=send, recv_sem=recv,
            device_id=where, device_id_type=MESH,
        )

    def arrived(ref, sem):
        pltpu.make_async_copy(ref, ref, sem).wait()

    def own_win(ref, h):
        return ref.at[pl.ds(half + 2 * h, 2)]

    def own_sum(ref, h):
        return ref.at[pl.ds(SUMB * b + 2 * (h - FIRST_SUM), 2)]

    def project(k, carry):
        w_copy(k).wait()
        full = jnp.dot(tok_v[...], w_v[k], preferred_element_type=F32)
        t0, t1, t2 = full[:, :PAIR], full[:, PAIR : 2 * PAIR], full[:, 2 * PAIR :]
        queries = pltpu.roll(jnp.where(low, t0, t1), HD, 1).astype(BF16) * BF16(HD**-0.5)
        ks[k] = jnp.where(low, t2, t0).astype(BF16).reshape(2, BLK, PAIR)
        values = jnp.where(low, t1, t2)
        for half_block in range(2):
            vs[k, half_block] = values[half_block * BLK : (half_block + 1) * BLK].T.astype(BF16)
        qs[k] = queries.reshape(2, BLK, PAIR)
        return carry

    def exchange(stage, send, recv, k, dst):
        return remote(stage.at[k], dst, send.at[k], recv.at[g], head=lax.rem(g + k, n_head))

    own_q = q_v.at[pl.ds(2 * g, 2)]

    def send_all(stage, send, recv, dst):
        for k in range(1, n_head):
            exchange(stage, send, recv, k, dst).start()
        pltpu.make_async_copy(stage.at[0], dst, recv.at[g]).start()

    def send_far_keys(k):
        @pl.when(summary_owner)
        def _():
            exchange(ks, k_send, k_recv, k, own_sum(sum_k, g)).start()

    def project_and_send(k, carry):
        project(k, carry)
        send_far_keys(k)
        return carry

    tok_copy.wait()
    early_groups = 3
    lax.fori_loop(1, 1 + early_groups, project, 0)
    pl.semaphore_wait(barrier, n_head - 1 + 4)
    for k in range(1, 1 + early_groups):
        send_far_keys(k)
    lax.fori_loop(1 + early_groups, n_head, project_and_send, 0)
    project(0, 0)

    @pl.when(summary_owner)
    def _():
        pltpu.make_async_copy(ks.at[0], own_sum(sum_k, g), k_recv.at[g]).start()
        send_all(vs, v_send, v_recv, own_sum(sum_v, g))

    @pl.when(jnp.logical_not(summary_owner))
    def _():
        send_all(qs, q_send, q_recv, own_q)

    def piece(kind, source, part):
        return ks_kinds[kind].at[pl.ds(SUMB * source + 2 * part, 2)]

    def dn_part(kind, n):
        part = lax.rem(n, chunks)
        return part if kind == 0 else chunks - 1 - part

    def up_copy(kind, n):
        ref = piece(kind, shifted(b, -2 * (n // chunks)), lax.rem(n, chunks))
        return remote(
            ref, ref, up_send.at[kind, n], up_recv.at[kind, n], blk=shifted(b, 2)
        )

    def dn_copy(kind, n):
        ref = piece(kind, shifted(b, 2 * (n // chunks)), dn_part(kind, n))
        return remote(
            ref, ref, dn_send.at[kind, n], dn_recv.at[kind, n], blk=shifted(b, -2)
        )

    def sib_copy(kind, m, ref):
        return remote(ref, ref, sib_send.at[kind, m], sib_recv.at[kind, m], blk=sibling)

    def start_own(kind):
        for part in range(chunks):
            ref = piece(kind, b, part)
            h = FIRST_SUM + part
            arrived(ref, (k_recv, v_recv)[kind].at[h])
            up_copy(kind, part).start()
            dn_copy(kind, part if kind == 0 else chunks - 1 - part).start()
            sib_copy(kind, part, ref).start()
            pltpu.make_async_copy(
                ref, own_win((win_k, win_v)[kind], h), loc_sem.at[kind, part]
            ).start()

    def relay(kind, n):
        ref = piece(kind, shifted(b, -2 * (n // chunks + 1)), lax.rem(n, chunks))
        arrived(ref, up_recv.at[kind, n])

        @pl.when(n < n_up[kind] - chunks)
        def _():
            up_copy(kind, n + chunks).start()

        sib_copy(kind, chunks + n, ref).start()

        @pl.when(n < n_dn[kind])
        def _():
            back = piece(kind, shifted(b, 2 * (n // chunks + 1)), dn_part(kind, n))
            arrived(back, dn_recv.at[kind, n])

            @pl.when(n < n_dn[kind] - chunks)
            def _():
                dn_copy(kind, n + chunks).start()

            sib_copy(kind, chunks + n_up[kind] + n, back).start()

    start_own(0)

    @pl.when(jnp.logical_not(summary_owner))
    def _():
        send_all(ks, k_send, k_recv, own_win(win_k, g))
        send_all(vs, v_send, v_recv, own_win(win_v, g))

    for n in range(chunks):
        relay(0, n)
    start_own(1)

    @pl.when(summary_owner)
    def _():
        send_all(qs, q_send, q_recv, own_q)

    lag = 4

    def relays(n, carry):
        relay(0, n)

        @pl.when(n >= lag)
        def _():
            relay(1, n - lag)

        return carry

    lax.fori_loop(chunks, n_up[0], relays, 0)

    early = chunks * (1 - core)

    def other_arrived(kind, m):
        s = sibling
        if kind == 0:
            down_part = lambda n: lax.rem(n, chunks)
        else:
            down_part = lambda n: chunks - 1 - lax.rem(n, chunks)

        @pl.when(m < chunks)
        def _():
            arrived(piece(kind, s, m), sib_recv.at[kind, m])

        n = m - chunks

        @pl.when(jnp.logical_and(n >= 0, n < n_up[kind]))
        def _():
            arrived(
                piece(kind, shifted(s, -2 * (n // chunks + 1)), lax.rem(n, chunks)),
                sib_recv.at[kind, m],
            )

        n2 = n - n_up[kind]

        @pl.when(n2 >= 0)
        def _():
            arrived(
                piece(kind, shifted(s, 2 * (n2 // chunks + 1)), down_part(n2)),
                sib_recv.at[kind, m],
            )

    def copy_below(kind):
        for part in range(chunks):
            other_arrived(kind, early + part)
            pltpu.make_async_copy(
                piece(kind, shifted(b, -1), part),
                (win_k, win_v)[kind].at[pl.ds(SUMB + 2 * part, 2)],
                loc_sem.at[kind, chunks + part],
            ).start()

    def others(kind):
        def body(m, carry):
            @pl.when(jnp.logical_or(m < early, m >= early + chunks))
            def _():
                other_arrived(kind, m)

            return carry

        lax.fori_loop(0, chunks * n_blk // 2, body, 0)

    def halo_place(ref, h):
        start = 3 * half + 2 * h if 2 * h < half else 2 * h - half
        return ref.at[pl.ds(start, 2)]

    def halo_copy(kind, h):
        ref = (win_k, win_v)[kind]
        shift = -1 if 2 * h < half else 1
        return remote(
            own_win(ref, h), halo_place(ref, h), halo_send.at[kind, h], halo_recv.at[kind, h],
            blk=shifted(b, shift),
        )

    for h in range(FIRST_SUM):
        for kind in range(2):
            arrived(own_win((win_k, win_v)[kind], h), (k_recv, v_recv)[kind].at[h])
            halo_copy(kind, h).start()
    copy_below(0)
    others(0)
    for h in range(n_head):
        arrived(q_v.at[pl.ds(2 * h, 2)], q_recv.at[h])
    pat_copy.wait()

    def masked_queries(i):
        block = q_v[i]
        zero = jnp.zeros_like(block)
        return jnp.concatenate([jnp.where(low, zero, block), jnp.where(low, block, zero)], axis=0)

    def scores_of(i, ref, places):
        keys = jnp.concatenate([ref[p] for p in places], axis=0)
        return lax.dot_general(
            keys, masked_queries(i), (((1,), (1,)), ((), ())), preferred_element_type=F32
        )

    ones = jnp.ones((16, BLK), BF16)

    def mixed(weights, ref, places):
        values = jnp.concatenate(
            [jnp.concatenate([ref[p], ones], axis=0) for p in places], axis=1
        )
        product = jnp.dot(values, weights, preferred_element_type=F32)
        return (
            (product[:HD, :BLK], product[HD:PAIR, BLK:]),
            product[PAIR : PAIR + 1],
        )

    def summary_places(i):
        places = []
        for j in range(LSEL, KSEL):
            block = pat_ref[i, j]
            within = jnp.maximum(lax.rem(block, SB) - (SB - SUMB), 0)
            places.append((block // SB) * SUMB + within)
        return places

    def summary_scores(i, buffer):
        scores = scores_of(i, sum_k, summary_places(i))
        buffer[...] = scores
        m_v[i] = jnp.broadcast_to(jnp.max(scores, axis=0, keepdims=True), (8, 2 * BLK))

    def summary_raise(i, buffer, top):
        p_v[i] = jnp.exp(buffer[...] - top).astype(BF16)

    def window_places(i):
        return [
            jnp.clip(pat_ref[i, j] - (SB * b - half), 0, SB + 2 * half - 1) for j in range(LSEL)
        ]

    near_rows = LSEL * BLK

    def window_scores(i, buffer):
        scores = scores_of(i, win_k, window_places(i))
        buffer[:near_rows] = scores
        near_m[i, :8] = jnp.broadcast_to(jnp.max(scores, axis=0, keepdims=True), (8, 2 * BLK))

    def window_mix(i, buffer, top):
        weights = jnp.exp(buffer[:near_rows] - top).astype(BF16)
        products, total = mixed(weights, win_v, window_places(i))
        near_v[i] = jnp.concatenate(products, axis=0)
        near_m[i, 8:] = jnp.broadcast_to(total, (8, 2 * BLK))

    def finish_block(i):
        products, far_total = mixed(p_v[i], sum_v, summary_places(i))
        far_top, near_top, near_total = m_v[i, :1], near_m[i, :1], near_m[i, 8:9]
        top = jnp.maximum(far_top, near_top)
        far, near = jnp.exp(far_top - top), jnp.exp(near_top - top)
        inverse = 1.0 / (far_total * far + near_total * near)
        far, near = far * inverse, near * inverse
        rows = []
        for which in range(2):
            lanes = slice(which * BLK, (which + 1) * BLK)
            near_part = near_v[i, which * HD : (which + 1) * HD]
            rows.append(products[which] * far[:, lanes] + near_part * near[:, lanes])
        return jnp.concatenate(rows, axis=0).T.astype(BF16)

    n_query = 2 * n_head

    def pipelined_pair(t, scores, use, tops):
        first, second = 2 * t, 2 * t + 1
        after = jnp.minimum(2 * t + 2, n_query - 1)
        top = tops[first, :1]
        scores(second, s_b)
        use(first, s_a, top)
        top = tops[second, :1]
        scores(after, s_a)
        use(second, s_b, top)

    summary_scores(0, s_a)

    def weights_pair(t, carry):
        pipelined_pair(t, summary_scores, summary_raise, m_v)

        @pl.when(t == 1)
        def _():
            relay(1, n_up[0] - lag + 0)

        @pl.when(t == 3)
        def _():
            relay(1, n_up[0] - lag + 1)

        @pl.when(t == 5)
        def _():
            relay(1, n_up[0] - lag + 2)

        return carry

    lax.fori_loop(0, n_head, weights_pair, 0)
    copy_below(1)
    for kind in range(2):
        ref = (win_k, win_v)[kind]
        for h in range(FIRST_SUM):
            arrived(halo_place(ref, h), halo_recv.at[kind, h])
        for part in range(chunks):
            arrived(own_win(ref, FIRST_SUM + part), loc_sem.at[kind, part])
            arrived(ref.at[pl.ds(SUMB + 2 * part, 2)], loc_sem.at[kind, chunks + part])

    window_scores(0, s_a)

    def window_pair(t, carry):
        pipelined_pair(t, window_scores, window_mix, near_m)
        return carry

    lax.fori_loop(0, n_head, window_pair, 0)
    others(1)

    columns = pl.ds(pl.multiple_of(g * PAIR, PAIR), PAIR)

    def out_to(t):
        dest = lax.rem(g + 1 + t, n_head)
        return remote(ost.at[t], attn.at[:, columns], out_send.at[t], out_recv.at[g], head=dest)

    def finish_pair(t, carry):
        dest = lax.rem(g + 1 + t, n_head)
        ost[t, :BLK] = finish_block(2 * dest)
        ost[t, BLK:] = finish_block(2 * dest + 1)

        @pl.when(t < n_head - 1)
        def _():
            out_to(t).start()

        return carry

    lax.fori_loop(0, n_head, finish_pair, 0)
    pltpu.make_async_copy(ost.at[n_head - 1], attn.at[:, columns], out_recv.at[g]).start()

    wo_copy.wait()
    for h in range(n_head):
        arrived(attn.at[:, pl.ds(h * PAIR, PAIR)], out_recv.at[h])
    out_ref[...] = jnp.dot(attn[...], wo_v[...], preferred_element_type=F32).astype(BF16)

    for k in range(1, n_head):
        exchange(ks, k_send, k_recv, k, own_q).wait_send()
        exchange(vs, v_send, v_recv, k, own_q).wait_send()
        exchange(qs, q_send, q_recv, k, own_q).wait_send()
        out_to(k - 1).wait_send()
    for kind in range(2):
        for h in range(FIRST_SUM):
            halo_copy(kind, h).wait_send()

        def sent(m, carry, kind=kind):
            sib_copy(kind, m, piece(kind, b, 0)).wait_send()

            @pl.when(m < n_up[kind])
            def _():
                up_copy(kind, m).wait_send()

            @pl.when(m < n_dn[kind])
            def _():
                dn_copy(kind, m).wait_send()

            return carry

        lax.fori_loop(0, chunks * n_blk // 2, sent, 0)


def on_device(n_head, n_blk, tokens, proj_weight, out_weight, pattern):
    rows = tokens.shape[1]
    n_query = pattern.shape[0]
    n_hop = SUMB * (n_blk // 8)
    n_sib = SUMB * (n_blk // 4)
    dma = pltpu.SemaphoreType.DMA
    blocks = lambda *lead: pltpu.VMEM((*lead, BLK, PAIR), BF16)
    out = pl.pallas_call(
        functools.partial(kernel, n_head, n_blk),
        out_shape=jax.ShapeDtypeStruct((rows, D), BF16),
        in_specs=[pl.BlockSpec(memory_space=pl.ANY)] * 4,
        out_specs=pl.BlockSpec(memory_space=pltpu.VMEM),
        scratch_shapes=[
            pltpu.VMEM((rows, D), BF16),
            pltpu.VMEM((n_head, D, 3 * PAIR), BF16),
            pltpu.VMEM((D, D), BF16),
            pltpu.SMEM((n_query, KSEL), jnp.int32),
            blocks(n_head, 2),
            blocks(n_head, 2),
            blocks(n_head, 2),
            blocks(SB + 2 * REACH),
            blocks(SB + 2 * REACH),
            blocks(SUMB * n_blk),
            blocks(SUMB * n_blk),
            blocks(n_query),
            pltpu.VMEM((n_query, 8, 2 * BLK), F32),
            pltpu.VMEM((n_query, SSEL * BLK, 2 * BLK), BF16),
            pltpu.VMEM((n_query, PAIR, BLK), F32),
            pltpu.VMEM((n_query, 16, 2 * BLK), F32),
            pltpu.VMEM((SSEL * BLK, 2 * BLK), F32),
            pltpu.VMEM((SSEL * BLK, 2 * BLK), F32),
            pltpu.VMEM((rows, D), BF16),
            pltpu.VMEM((n_head, rows, PAIR), BF16),
            dma((3,)),
            dma((n_head,)),
            dma((n_head,)),
            dma((n_head,)),
            dma((n_head,)),
            dma((n_head,)),
            dma((n_head,)),
            dma((n_head,)),
            dma((2, n_hop)),
            dma((2, n_hop)),
            dma((2, n_hop)),
            dma((2, n_hop)),
            dma((2, n_sib)),
            dma((2, n_sib)),
            dma((2, FIRST_SUM)),
            dma((2, FIRST_SUM)),
            dma((2, SUMB)),
            dma((n_head,)),
            dma((n_head,)),
        ],
        compiler_params=pltpu.CompilerParams(
            collective_id=0, has_side_effects=True, vmem_limit_bytes=53 * 1024 * 1024
        ),
    )(tokens[0], proj_weight, out_weight, pattern)
    return out.reshape(1, rows, D)


def solution(mesh):
    return jax.shard_map(
        functools.partial(on_device, mesh.shape["head"], mesh.shape["blk"]),
        mesh=mesh,
        in_specs=(P(("batch", "blk"), "head", None), P(), P(), P(("batch", "blk"), None)),
        out_specs=P(("batch", "blk"), "head", None),
        check_vma=False,
    )
```

```python
import functools

import jax
import jax.numpy as jnp
from jax import lax
from jax.experimental import pallas as pl
from jax.experimental.pallas import tpu as pltpu
from jax.sharding import PartitionSpec as P

D = 1024
H = 16
HD = 64
BLK = 128
KSEL = 16
LSEL = 6
SSEL = 10
SB = 16
REACH = 8
SUMB = 4
MESH = pl.DeviceIdType.MESH
F32 = jnp.float32
BF16 = jnp.bfloat16
PAIR = 2 * HD
FIRST_SUM = (SB - SUMB) // 2


def kernel(
    n_head, n_blk, tok_hbm, w_hbm, wo_hbm, pat_hbm, out_ref,
    tok_v, w_v, wo_v, pat_ref, ks, vs, qs, win_k, win_v, sum_k, sum_v,
    q_v, m_v, p_v, near_v, near_m, s_a, s_b, attn, ost,
    in_sem, w_sem, k_send, k_recv, v_send, v_recv, q_send, q_recv,
    up_send, up_recv, dn_send, dn_recv, sib_send, sib_recv,
    halo_send, halo_recv, loc_sem, out_send, out_recv,
):
    g = lax.axis_index("head")
    b = lax.axis_index("blk")
    core = lax.rem(b, 2)
    sibling = b + 1 - 2 * core
    half = REACH
    chunks = SUMB // 2
    summary_owner = g >= FIRST_SUM
    ks_kinds = (sum_k, sum_v)
    steps = n_blk // 4
    n_up = (chunks * steps, chunks * steps - 1)
    n_dn = (chunks * (steps - 1), chunks * (steps - 1) + 1)

    def shifted(position, shift):
        return lax.rem(position + n_blk + shift, n_blk)

    def w_copy(k):
        dest = lax.rem(g + k, n_head)
        col = pl.multiple_of(dest * (3 * PAIR), PAIR)
        return pltpu.make_async_copy(w_hbm.at[:, pl.ds(col, 3 * PAIR)], w_v.at[k], w_sem.at[k])

    tok_copy = pltpu.make_async_copy(tok_hbm, tok_v, in_sem.at[0])
    wo_copy = pltpu.make_async_copy(wo_hbm, wo_v, in_sem.at[1])
    pat_copy = pltpu.make_async_copy(pat_hbm, pat_ref, in_sem.at[2])
    tok_copy.start()
    for k in range(n_head):
        w_copy((k + 1) % n_head).start()
    pat_copy.start()
    wo_copy.start()

    barrier = pltpu.get_barrier_semaphore()
    for k in range(1, n_head):
        pl.semaphore_signal(
            barrier, inc=1, device_id={"head": lax.rem(g + k, n_head)}, device_id_type=MESH
        )
    for shift in (-2, -1, 1, 2):
        pl.semaphore_signal(
            barrier, inc=1, device_id={"blk": shifted(b, shift)}, device_id_type=MESH
        )

    low = lax.broadcasted_iota(jnp.int32, (1, PAIR), 1) < HD

    def remote(src, dst, send, recv, **where):
        return pltpu.make_async_remote_copy(
            src_ref=src, dst_ref=dst, send_sem=send, recv_sem=recv,
            device_id=where, device_id_type=MESH,
        )

    def arrived(ref, sem):
        pltpu.make_async_copy(ref, ref, sem).wait()

    def own_win(ref, h):
        return ref.at[pl.ds(half + 2 * h, 2)]

    def own_sum(ref, h):
        return ref.at[pl.ds(SUMB * b + 2 * (h - FIRST_SUM), 2)]

    def project(k, carry):
        w_copy(k).wait()
        full = jnp.dot(tok_v[...], w_v[k], preferred_element_type=F32)
        t0, t1, t2 = full[:, :PAIR], full[:, PAIR : 2 * PAIR], full[:, 2 * PAIR :]
        queries = pltpu.roll(jnp.where(low, t0, t1), HD, 1).astype(BF16) * BF16(HD**-0.5)
        ks[k] = jnp.where(low, t2, t0).astype(BF16).reshape(2, BLK, PAIR)
        values = jnp.where(low, t1, t2)
        for half_block in range(2):
            vs[k, half_block] = values[half_block * BLK : (half_block + 1) * BLK].T.astype(BF16)
        qs[k] = queries.reshape(2, BLK, PAIR)
        return carry

    def exchange(stage, send, recv, k, dst):
        return remote(stage.at[k], dst, send.at[k], recv.at[g], head=lax.rem(g + k, n_head))

    own_q = q_v.at[pl.ds(2 * g, 2)]

    def send_all(stage, send, recv, dst):
        for k in range(1, n_head):
            exchange(stage, send, recv, k, dst).start()
        pltpu.make_async_copy(stage.at[0], dst, recv.at[g]).start()

    def send_far_keys(k):
        @pl.when(summary_owner)
        def _():
            exchange(ks, k_send, k_recv, k, own_sum(sum_k, g)).start()

    def project_and_send(k, carry):
        project(k, carry)
        send_far_keys(k)
        return carry

    tok_copy.wait()
    early_groups = 3
    lax.fori_loop(1, 1 + early_groups, project, 0)
    pl.semaphore_wait(barrier, n_head - 1 + 4)
    for k in range(1, 1 + early_groups):
        send_far_keys(k)
    lax.fori_loop(1 + early_groups, n_head, project_and_send, 0)
    project(0, 0)

    @pl.when(summary_owner)
    def _():
        pltpu.make_async_copy(ks.at[0], own_sum(sum_k, g), k_recv.at[g]).start()
        send_all(vs, v_send, v_recv, own_sum(sum_v, g))

    @pl.when(jnp.logical_not(summary_owner))
    def _():
        send_all(ks, k_send, k_recv, own_win(win_k, g))
        send_all(vs, v_send, v_recv, own_win(win_v, g))

    def piece(kind, source, part):
        return ks_kinds[kind].at[pl.ds(SUMB * source + 2 * part, 2)]

    def dn_part(kind, n):
        part = lax.rem(n, chunks)
        return part if kind == 0 else chunks - 1 - part

    def up_copy(kind, n):
        ref = piece(kind, shifted(b, -2 * (n // chunks)), lax.rem(n, chunks))
        return remote(
            ref, ref, up_send.at[kind, n], up_recv.at[kind, n], blk=shifted(b, 2)
        )

    def dn_copy(kind, n):
        ref = piece(kind, shifted(b, 2 * (n // chunks)), dn_part(kind, n))
        return remote(
            ref, ref, dn_send.at[kind, n], dn_recv.at[kind, n], blk=shifted(b, -2)
        )

    def sib_copy(kind, m, ref):
        return remote(ref, ref, sib_send.at[kind, m], sib_recv.at[kind, m], blk=sibling)

    def start_own(kind):
        for part in range(chunks):
            ref = piece(kind, b, part)
            h = FIRST_SUM + part
            arrived(ref, (k_recv, v_recv)[kind].at[h])
            up_copy(kind, part).start()
            dn_copy(kind, part if kind == 0 else chunks - 1 - part).start()
            sib_copy(kind, part, ref).start()
            pltpu.make_async_copy(
                ref, own_win((win_k, win_v)[kind], h), loc_sem.at[kind, part]
            ).start()

    def relay(kind, n):
        ref = piece(kind, shifted(b, -2 * (n // chunks + 1)), lax.rem(n, chunks))
        arrived(ref, up_recv.at[kind, n])

        @pl.when(n < n_up[kind] - chunks)
        def _():
            up_copy(kind, n + chunks).start()

        sib_copy(kind, chunks + n, ref).start()

        @pl.when(n < n_dn[kind])
        def _():
            back = piece(kind, shifted(b, 2 * (n // chunks + 1)), dn_part(kind, n))
            arrived(back, dn_recv.at[kind, n])

            @pl.when(n < n_dn[kind] - chunks)
            def _():
                dn_copy(kind, n + chunks).start()

            sib_copy(kind, chunks + n_up[kind] + n, back).start()

    start_own(0)

    @pl.when(jnp.logical_not(summary_owner))
    def _():
        send_all(qs, q_send, q_recv, own_q)

    for n in range(chunks):
        relay(0, n)
    start_own(1)

    @pl.when(summary_owner)
    def _():
        send_all(qs, q_send, q_recv, own_q)

    lag = 4

    def relays(n, carry):
        relay(0, n)

        @pl.when(n >= lag)
        def _():
            relay(1, n - lag)

        return carry

    def halo_place(ref, h):
        start = 3 * half + 2 * h if 2 * h < half else 2 * h - half
        return ref.at[pl.ds(start, 2)]

    def halo_copy(kind, h):
        ref = (win_k, win_v)[kind]
        shift = -1 if 2 * h < half else 1
        return remote(
            own_win(ref, h), halo_place(ref, h), halo_send.at[kind, h], halo_recv.at[kind, h],
            blk=shifted(b, shift),
        )

    lax.fori_loop(chunks, 6, relays, 0)
    for h in range(FIRST_SUM):
        for kind in range(2):
            arrived(own_win((win_k, win_v)[kind], h), (k_recv, v_recv)[kind].at[h])
            halo_copy(kind, h).start()
    lax.fori_loop(6, n_up[0], relays, 0)

    early = chunks * (1 - core)

    def other_arrived(kind, m):
        s = sibling
        if kind == 0:
            down_part = lambda n: lax.rem(n, chunks)
        else:
            down_part = lambda n: chunks - 1 - lax.rem(n, chunks)

        @pl.when(m < chunks)
        def _():
            arrived(piece(kind, s, m), sib_recv.at[kind, m])

        n = m - chunks

        @pl.when(jnp.logical_and(n >= 0, n < n_up[kind]))
        def _():
            arrived(
                piece(kind, shifted(s, -2 * (n // chunks + 1)), lax.rem(n, chunks)),
                sib_recv.at[kind, m],
            )

        n2 = n - n_up[kind]

        @pl.when(n2 >= 0)
        def _():
            arrived(
                piece(kind, shifted(s, 2 * (n2 // chunks + 1)), down_part(n2)),
                sib_recv.at[kind, m],
            )

    def copy_below(kind):
        for part in range(chunks):
            other_arrived(kind, early + part)
            pltpu.make_async_copy(
                piece(kind, shifted(b, -1), part),
                (win_k, win_v)[kind].at[pl.ds(SUMB + 2 * part, 2)],
                loc_sem.at[kind, chunks + part],
            ).start()

    def others(kind):
        def body(m, carry):
            @pl.when(jnp.logical_or(m < early, m >= early + chunks))
            def _():
                other_arrived(kind, m)

            return carry

        lax.fori_loop(0, chunks * n_blk // 2, body, 0)

    copy_below(0)
    others(0)
    for h in range(n_head):
        arrived(q_v.at[pl.ds(2 * h, 2)], q_recv.at[h])
    pat_copy.wait()

    def masked_queries(i):
        block = q_v[i]
        zero = jnp.zeros_like(block)
        return jnp.concatenate([jnp.where(low, zero, block), jnp.where(low, block, zero)], axis=0)

    def scores_of(i, ref, places):
        keys = jnp.concatenate([ref[p] for p in places], axis=0)
        return lax.dot_general(
            keys, masked_queries(i), (((1,), (1,)), ((), ())), preferred_element_type=F32
        )

    ones = jnp.ones((16, BLK), BF16)

    def mixed(weights, ref, places):
        values = jnp.concatenate(
            [jnp.concatenate([ref[p], ones], axis=0) for p in places], axis=1
        )
        product = jnp.dot(values, weights, preferred_element_type=F32)
        return (
            (product[:HD, :BLK], product[HD:PAIR, BLK:]),
            product[PAIR : PAIR + 1],
        )

    def summary_places(i):
        places = []
        for j in range(LSEL, KSEL):
            block = pat_ref[i, j]
            within = jnp.maximum(lax.rem(block, SB) - (SB - SUMB), 0)
            places.append((block // SB) * SUMB + within)
        return places

    def summary_scores(i, buffer):
        scores = scores_of(i, sum_k, summary_places(i))
        buffer[...] = scores
        m_v[i] = jnp.broadcast_to(jnp.max(scores, axis=0, keepdims=True), (8, 2 * BLK))

    def summary_raise(i, buffer, top):
        p_v[i] = jnp.exp(buffer[...] - top).astype(BF16)

    def window_places(i):
        return [
            jnp.clip(pat_ref[i, j] - (SB * b - half), 0, SB + 2 * half - 1) for j in range(LSEL)
        ]

    near_rows = LSEL * BLK

    def window_scores(i, buffer):
        scores = scores_of(i, win_k, window_places(i))
        buffer[:near_rows] = scores
        near_m[i, :8] = jnp.broadcast_to(jnp.max(scores, axis=0, keepdims=True), (8, 2 * BLK))

    def window_mix(i, buffer, top):
        weights = jnp.exp(buffer[:near_rows] - top).astype(BF16)
        products, total = mixed(weights, win_v, window_places(i))
        near_v[i] = jnp.concatenate(products, axis=0)
        near_m[i, 8:] = jnp.broadcast_to(total, (8, 2 * BLK))

    def finish_block(i):
        products, far_total = mixed(p_v[i], sum_v, summary_places(i))
        far_top, near_top, near_total = m_v[i, :1], near_m[i, :1], near_m[i, 8:9]
        top = jnp.maximum(far_top, near_top)
        far, near = jnp.exp(far_top - top), jnp.exp(near_top - top)
        inverse = 1.0 / (far_total * far + near_total * near)
        far, near = far * inverse, near * inverse
        rows = []
        for which in range(2):
            lanes = slice(which * BLK, (which + 1) * BLK)
            near_part = near_v[i, which * HD : (which + 1) * HD]
            rows.append(products[which] * far[:, lanes] + near_part * near[:, lanes])
        return jnp.concatenate(rows, axis=0).T.astype(BF16)

    n_query = 2 * n_head

    def pipelined_pair(t, scores, use, tops):
        first, second = 2 * t, 2 * t + 1
        after = jnp.minimum(2 * t + 2, n_query - 1)
        top = tops[first, :1]
        scores(second, s_b)
        use(first, s_a, top)
        top = tops[second, :1]
        scores(after, s_a)
        use(second, s_b, top)

    summary_scores(0, s_a)

    def weights_pair(t, carry):
        pipelined_pair(t, summary_scores, summary_raise, m_v)

        @pl.when(t == 1)
        def _():
            relay(1, n_up[0] - lag + 0)

        @pl.when(t == 3)
        def _():
            relay(1, n_up[0] - lag + 1)

        @pl.when(t == 5)
        def _():
            relay(1, n_up[0] - lag + 2)

        return carry

    lax.fori_loop(0, n_head, weights_pair, 0)
    copy_below(1)
    for kind in range(2):
        ref = (win_k, win_v)[kind]
        for h in range(FIRST_SUM):
            arrived(halo_place(ref, h), halo_recv.at[kind, h])
        for part in range(chunks):
            arrived(own_win(ref, FIRST_SUM + part), loc_sem.at[kind, part])
            arrived(ref.at[pl.ds(SUMB + 2 * part, 2)], loc_sem.at[kind, chunks + part])

    window_scores(0, s_a)

    def window_pair(t, carry):
        pipelined_pair(t, window_scores, window_mix, near_m)
        return carry

    lax.fori_loop(0, n_head, window_pair, 0)
    others(1)

    def out_dest(t):
        return lax.rem(g + 2 * t + 1 - (n_head - 1) * (t // (n_head // 2)), n_head)

    def out_to(t):
        dest = out_dest(t)
        return remote(ost.at[t], attn.at[g], out_send.at[t], out_recv.at[g], head=dest)

    def finish_pair(t, carry):
        dest = out_dest(t)
        ost[t, :BLK] = finish_block(2 * dest)
        ost[t, BLK:] = finish_block(2 * dest + 1)

        @pl.when(t < n_head - 1)
        def _():
            out_to(t).start()

        return carry

    lax.fori_loop(0, n_head, finish_pair, 0)
    pltpu.make_async_copy(ost.at[n_head - 1], attn.at[g], out_recv.at[g]).start()

    wo_copy.wait()
    for h in range(n_head):
        arrived(attn.at[h], out_recv.at[h])
    heads = jnp.concatenate([attn[h] for h in range(n_head)], axis=1)
    out_ref[...] = jnp.dot(heads, wo_v[...], preferred_element_type=F32).astype(BF16)

    for k in range(1, n_head):
        exchange(ks, k_send, k_recv, k, own_q).wait_send()
        exchange(vs, v_send, v_recv, k, own_q).wait_send()
        exchange(qs, q_send, q_recv, k, own_q).wait_send()
        out_to(k - 1).wait_send()
    for kind in range(2):
        for h in range(FIRST_SUM):
            halo_copy(kind, h).wait_send()

        def sent(m, carry, kind=kind):
            sib_copy(kind, m, piece(kind, b, 0)).wait_send()

            @pl.when(m < n_up[kind])
            def _():
                up_copy(kind, m).wait_send()

            @pl.when(m < n_dn[kind])
            def _():
                dn_copy(kind, m).wait_send()

            return carry

        lax.fori_loop(0, chunks * n_blk // 2, sent, 0)


def on_device(n_head, n_blk, tokens, proj_weight, out_weight, pattern):
    rows = tokens.shape[1]
    n_query = pattern.shape[0]
    n_hop = SUMB * (n_blk // 8)
    n_sib = SUMB * (n_blk // 4)
    dma = pltpu.SemaphoreType.DMA
    blocks = lambda *lead: pltpu.VMEM((*lead, BLK, PAIR), BF16)
    out = pl.pallas_call(
        functools.partial(kernel, n_head, n_blk),
        out_shape=jax.ShapeDtypeStruct((rows, D), BF16),
        in_specs=[pl.BlockSpec(memory_space=pl.ANY)] * 4,
        out_specs=pl.BlockSpec(memory_space=pltpu.VMEM),
        scratch_shapes=[
            pltpu.VMEM((rows, D), BF16),
            pltpu.VMEM((n_head, D, 3 * PAIR), BF16),
            pltpu.VMEM((D, D), BF16),
            pltpu.SMEM((n_query, KSEL), jnp.int32),
            blocks(n_head, 2),
            blocks(n_head, 2),
            blocks(n_head, 2),
            blocks(SB + 2 * REACH),
            blocks(SB + 2 * REACH),
            blocks(SUMB * n_blk),
            blocks(SUMB * n_blk),
            blocks(n_query),
            pltpu.VMEM((n_query, 8, 2 * BLK), F32),
            pltpu.VMEM((n_query, SSEL * BLK, 2 * BLK), BF16),
            pltpu.VMEM((n_query, PAIR, BLK), F32),
            pltpu.VMEM((n_query, 16, 2 * BLK), F32),
            pltpu.VMEM((SSEL * BLK, 2 * BLK), F32),
            pltpu.VMEM((SSEL * BLK, 2 * BLK), F32),
            pltpu.VMEM((n_head, rows, PAIR), BF16),
            pltpu.VMEM((n_head, rows, PAIR), BF16),
            dma((3,)),
            dma((n_head,)),
            dma((n_head,)),
            dma((n_head,)),
            dma((n_head,)),
            dma((n_head,)),
            dma((n_head,)),
            dma((n_head,)),
            dma((2, n_hop)),
            dma((2, n_hop)),
            dma((2, n_hop)),
            dma((2, n_hop)),
            dma((2, n_sib)),
            dma((2, n_sib)),
            dma((2, FIRST_SUM)),
            dma((2, FIRST_SUM)),
            dma((2, SUMB)),
            dma((n_head,)),
            dma((n_head,)),
        ],
        compiler_params=pltpu.CompilerParams(
            collective_id=0, has_side_effects=True, vmem_limit_bytes=53 * 1024 * 1024
        ),
    )(tokens[0], proj_weight, out_weight, pattern)
    return out.reshape(1, rows, D)


def solution(mesh):
    return jax.shard_map(
        functools.partial(on_device, mesh.shape["head"], mesh.shape["blk"]),
        mesh=mesh,
        in_specs=(P(("batch", "blk"), "head", None), P(), P(), P(("batch", "blk"), None)),
        out_specs=P(("batch", "blk"), "head", None),
        check_vma=False,
    )
```

```python
import functools

import jax
import jax.numpy as jnp
from jax import lax
from jax.experimental import pallas as pl
from jax.experimental.pallas import tpu as pltpu
from jax.sharding import PartitionSpec as P

D = 1024
H = 16
HD = 64
BLK = 128
KSEL = 16
LSEL = 6
SSEL = 10
SB = 16
REACH = 8
SUMB = 4
MESH = pl.DeviceIdType.MESH
F32 = jnp.float32
BF16 = jnp.bfloat16
PAIR = 2 * HD
FIRST_SUM = (SB - SUMB) // 2


def kernel(
    n_head, n_blk, tok_hbm, w_hbm, wo_hbm, pat_hbm, out_ref,
    tok_v, w_v, wo_v, pat_ref, ks, vs, qs, win_k, win_v, sum_k, sum_v,
    q_v, m_v, p_v, near_v, near_m, s_a, s_b, attn, ost,
    in_sem, w_sem, k_send, k_recv, v_send, v_recv, q_send, q_recv,
    up_send, up_recv, dn_send, dn_recv, sib_send, sib_recv,
    halo_send, halo_recv, loc_sem, out_send, out_recv,
):
    g = lax.axis_index("head")
    b = lax.axis_index("blk")
    core = lax.rem(b, 2)
    sibling = b + 1 - 2 * core
    half = REACH
    chunks = SUMB // 2
    summary_owner = g >= FIRST_SUM
    ks_kinds = (sum_k, sum_v)
    steps = n_blk // 4
    n_up = (chunks * steps, chunks * steps - 1)
    n_dn = (chunks * (steps - 1), chunks * (steps - 1) + 1)

    def shifted(position, shift):
        return lax.rem(position + n_blk + shift, n_blk)

    def w_copy(k):
        dest = lax.rem(g + k, n_head)
        col = pl.multiple_of(dest * (3 * PAIR), PAIR)
        return pltpu.make_async_copy(w_hbm.at[:, pl.ds(col, 3 * PAIR)], w_v.at[k], w_sem.at[k])

    tok_copy = pltpu.make_async_copy(tok_hbm, tok_v, in_sem.at[0])
    wo_copy = pltpu.make_async_copy(wo_hbm, wo_v, in_sem.at[1])
    pat_copy = pltpu.make_async_copy(pat_hbm, pat_ref, in_sem.at[2])
    tok_copy.start()
    for k in range(n_head):
        w_copy((k + 1) % n_head).start()
    pat_copy.start()
    wo_copy.start()

    barrier = pltpu.get_barrier_semaphore()
    for k in range(1, n_head):
        pl.semaphore_signal(
            barrier, inc=1, device_id={"head": lax.rem(g + k, n_head)}, device_id_type=MESH
        )
    for shift in (-2, -1, 1, 2):
        pl.semaphore_signal(
            barrier, inc=1, device_id={"blk": shifted(b, shift)}, device_id_type=MESH
        )

    low = lax.broadcasted_iota(jnp.int32, (1, PAIR), 1) < HD

    def remote(src, dst, send, recv, **where):
        return pltpu.make_async_remote_copy(
            src_ref=src, dst_ref=dst, send_sem=send, recv_sem=recv,
            device_id=where, device_id_type=MESH,
        )

    def arrived(ref, sem):
        pltpu.make_async_copy(ref, ref, sem).wait()

    def own_win(ref, h):
        return ref.at[pl.ds(half + 2 * h, 2)]

    def own_sum(ref, h):
        return ref.at[pl.ds(SUMB * b + 2 * (h - FIRST_SUM), 2)]

    def project(k, carry):
        w_copy(k).wait()
        full = jnp.dot(tok_v[...], w_v[k], preferred_element_type=F32)
        t0, t1, t2 = full[:, :PAIR], full[:, PAIR : 2 * PAIR], full[:, 2 * PAIR :]
        queries = pltpu.roll(jnp.where(low, t0, t1), HD, 1).astype(BF16) * BF16(HD**-0.5)
        ks[k] = jnp.where(low, t2, t0).astype(BF16).reshape(2, BLK, PAIR)
        values = jnp.where(low, t1, t2)
        for half_block in range(2):
            vs[k, half_block] = values[half_block * BLK : (half_block + 1) * BLK].T.astype(BF16)
        qs[k] = queries.reshape(2, BLK, PAIR)
        return carry

    def exchange(stage, send, recv, k, dst):
        return remote(stage.at[k], dst, send.at[k], recv.at[g], head=lax.rem(g + k, n_head))

    own_q = q_v.at[pl.ds(2 * g, 2)]

    def send_all(stage, send, recv, dst):
        for k in range(1, n_head):
            exchange(stage, send, recv, k, dst).start()
        pltpu.make_async_copy(stage.at[0], dst, recv.at[g]).start()

    def send_far_keys(k):
        @pl.when(summary_owner)
        def _():
            exchange(ks, k_send, k_recv, k, own_sum(sum_k, g)).start()

    def project_and_send(k, carry):
        project(k, carry)
        send_far_keys(k)
        return carry

    tok_copy.wait()
    early_groups = 3
    lax.fori_loop(1, 1 + early_groups, project, 0)
    pl.semaphore_wait(barrier, n_head - 1 + 4)
    for k in range(1, 1 + early_groups):
        send_far_keys(k)
    lax.fori_loop(1 + early_groups, n_head, project_and_send, 0)
    project(0, 0)

    @pl.when(summary_owner)
    def _():
        pltpu.make_async_copy(ks.at[0], own_sum(sum_k, g), k_recv.at[g]).start()
        send_all(vs, v_send, v_recv, own_sum(sum_v, g))

    @pl.when(jnp.logical_not(summary_owner))
    def _():
        send_all(ks, k_send, k_recv, own_win(win_k, g))
        send_all(vs, v_send, v_recv, own_win(win_v, g))

    def piece(kind, source, part):
        return ks_kinds[kind].at[pl.ds(SUMB * source + 2 * part, 2)]

    def dn_part(kind, n):
        part = lax.rem(n, chunks)
        return part if kind == 0 else chunks - 1 - part

    def up_copy(kind, n):
        ref = piece(kind, shifted(b, -2 * (n // chunks)), lax.rem(n, chunks))
        return remote(
            ref, ref, up_send.at[kind, n], up_recv.at[kind, n], blk=shifted(b, 2)
        )

    def dn_copy(kind, n):
        ref = piece(kind, shifted(b, 2 * (n // chunks)), dn_part(kind, n))
        return remote(
            ref, ref, dn_send.at[kind, n], dn_recv.at[kind, n], blk=shifted(b, -2)
        )

    def sib_copy(kind, m, ref):
        return remote(ref, ref, sib_send.at[kind, m], sib_recv.at[kind, m], blk=sibling)

    def start_own(kind):
        for part in range(chunks):
            ref = piece(kind, b, part)
            h = FIRST_SUM + part
            arrived(ref, (k_recv, v_recv)[kind].at[h])
            up_copy(kind, part).start()
            dn_copy(kind, part if kind == 0 else chunks - 1 - part).start()
            sib_copy(kind, part, ref).start()
            pltpu.make_async_copy(
                ref, own_win((win_k, win_v)[kind], h), loc_sem.at[kind, part]
            ).start()

    def relay(kind, n):
        ref = piece(kind, shifted(b, -2 * (n // chunks + 1)), lax.rem(n, chunks))
        arrived(ref, up_recv.at[kind, n])

        @pl.when(n < n_up[kind] - chunks)
        def _():
            up_copy(kind, n + chunks).start()

        sib_copy(kind, chunks + n, ref).start()

        @pl.when(n < n_dn[kind])
        def _():
            back = piece(kind, shifted(b, 2 * (n // chunks + 1)), dn_part(kind, n))
            arrived(back, dn_recv.at[kind, n])

            @pl.when(n < n_dn[kind] - chunks)
            def _():
                dn_copy(kind, n + chunks).start()

            sib_copy(kind, chunks + n_up[kind] + n, back).start()

    start_own(0)

    @pl.when(jnp.logical_not(summary_owner))
    def _():
        send_all(qs, q_send, q_recv, own_q)

    for n in range(chunks):
        relay(0, n)
    start_own(1)

    @pl.when(summary_owner)
    def _():
        send_all(qs, q_send, q_recv, own_q)

    lag = 4

    def relays(n, carry):
        relay(0, n)

        @pl.when(n >= lag)
        def _():
            relay(1, n - lag)

        return carry

    def halo_place(ref, h):
        start = 3 * half + 2 * h if 2 * h < half else 2 * h - half
        return ref.at[pl.ds(start, 2)]

    def halo_copy(kind, h):
        ref = (win_k, win_v)[kind]
        shift = -1 if 2 * h < half else 1
        return remote(
            own_win(ref, h), halo_place(ref, h), halo_send.at[kind, h], halo_recv.at[kind, h],
            blk=shifted(b, shift),
        )

    lax.fori_loop(chunks, 6, relays, 0)
    for h in range(FIRST_SUM):
        for kind in range(2):
            arrived(own_win((win_k, win_v)[kind], h), (k_recv, v_recv)[kind].at[h])
            halo_copy(kind, h).start()
    lax.fori_loop(6, n_up[0], relays, 0)

    early = chunks * (1 - core)

    def other_arrived(kind, m):
        s = sibling
        if kind == 0:
            down_part = lambda n: lax.rem(n, chunks)
        else:
            down_part = lambda n: chunks - 1 - lax.rem(n, chunks)

        @pl.when(m < chunks)
        def _():
            arrived(piece(kind, s, m), sib_recv.at[kind, m])

        n = m - chunks

        @pl.when(jnp.logical_and(n >= 0, n < n_up[kind]))
        def _():
            arrived(
                piece(kind, shifted(s, -2 * (n // chunks + 1)), lax.rem(n, chunks)),
                sib_recv.at[kind, m],
            )

        n2 = n - n_up[kind]

        @pl.when(n2 >= 0)
        def _():
            arrived(
                piece(kind, shifted(s, 2 * (n2 // chunks + 1)), down_part(n2)),
                sib_recv.at[kind, m],
            )

    def copy_below(kind):
        for part in range(chunks):
            other_arrived(kind, early + part)
            pltpu.make_async_copy(
                piece(kind, shifted(b, -1), part),
                (win_k, win_v)[kind].at[pl.ds(SUMB + 2 * part, 2)],
                loc_sem.at[kind, chunks + part],
            ).start()

    def others(kind):
        def body(m, carry):
            @pl.when(jnp.logical_or(m < early, m >= early + chunks))
            def _():
                other_arrived(kind, m)

            return carry

        lax.fori_loop(0, chunks * n_blk // 2, body, 0)

    copy_below(0)
    others(0)
    for h in range(n_head):
        arrived(q_v.at[pl.ds(2 * h, 2)], q_recv.at[h])
    pat_copy.wait()

    def masked_queries(i):
        block = q_v[i]
        zero = jnp.zeros_like(block)
        return jnp.concatenate([jnp.where(low, zero, block), jnp.where(low, block, zero)], axis=0)

    def scores_of(i, ref, places):
        keys = jnp.concatenate([ref[p] for p in places], axis=0)
        return lax.dot_general(
            keys, masked_queries(i), (((1,), (1,)), ((), ())), preferred_element_type=F32
        )

    ones = jnp.ones((16, BLK), BF16)

    def mixed(weights, ref, places):
        values = jnp.concatenate(
            [jnp.concatenate([ref[p], ones], axis=0) for p in places], axis=1
        )
        product = jnp.dot(values, weights, preferred_element_type=F32)
        return (
            (product[:HD, :BLK], product[HD:PAIR, BLK:]),
            product[PAIR : PAIR + 1],
        )

    def summary_places(i):
        places = []
        for j in range(LSEL, KSEL):
            block = pat_ref[i, j]
            within = jnp.maximum(lax.rem(block, SB) - (SB - SUMB), 0)
            places.append((block // SB) * SUMB + within)
        return places

    def summary_scores(i, buffer):
        scores = scores_of(i, sum_k, summary_places(i))
        buffer[...] = scores
        m_v[i] = jnp.broadcast_to(jnp.max(scores, axis=0, keepdims=True), (8, 2 * BLK))

    def summary_raise(i, buffer, top):
        p_v[i] = jnp.exp(buffer[...] - top).astype(BF16)

    def window_places(i):
        return [
            jnp.clip(pat_ref[i, j] - (SB * b - half), 0, SB + 2 * half - 1) for j in range(LSEL)
        ]

    near_rows = LSEL * BLK

    def window_scores(i, buffer):
        scores = scores_of(i, win_k, window_places(i))
        buffer[:near_rows] = scores
        near_m[i, :8] = jnp.broadcast_to(jnp.max(scores, axis=0, keepdims=True), (8, 2 * BLK))

    def window_mix(i, buffer, top):
        weights = jnp.exp(buffer[:near_rows] - top).astype(BF16)
        products, total = mixed(weights, win_v, window_places(i))
        near_v[i] = jnp.concatenate(products, axis=0)
        near_m[i, 8:] = jnp.broadcast_to(total, (8, 2 * BLK))

    def finish_block(i):
        products, far_total = mixed(p_v[i], sum_v, summary_places(i))
        far_top, near_top, near_total = m_v[i, :1], near_m[i, :1], near_m[i, 8:9]
        top = jnp.maximum(far_top, near_top)
        far, near = jnp.exp(far_top - top), jnp.exp(near_top - top)
        inverse = 1.0 / (far_total * far + near_total * near)
        far, near = far * inverse, near * inverse
        rows = []
        for which in range(2):
            lanes = slice(which * BLK, (which + 1) * BLK)
            near_part = near_v[i, which * HD : (which + 1) * HD]
            rows.append(products[which] * far[:, lanes] + near_part * near[:, lanes])
        return jnp.concatenate(rows, axis=0).T.astype(BF16)

    n_query = 2 * n_head

    def pipelined_pair(t, scores, use, tops):
        first, second = 2 * t, 2 * t + 1
        after = jnp.minimum(2 * t + 2, n_query - 1)
        top = tops[first, :1]
        scores(second, s_b)
        use(first, s_a, top)
        top = tops[second, :1]
        scores(after, s_a)
        use(second, s_b, top)

    summary_scores(0, s_a)

    def weights_pair(t, carry):
        pipelined_pair(t, summary_scores, summary_raise, m_v)

        @pl.when(t == 1)
        def _():
            relay(1, n_up[0] - lag + 0)

        @pl.when(t == 3)
        def _():
            relay(1, n_up[0] - lag + 1)

        @pl.when(t == 5)
        def _():
            relay(1, n_up[0] - lag + 2)

        return carry

    lax.fori_loop(0, n_head, weights_pair, 0)
    copy_below(1)
    for kind in range(2):
        ref = (win_k, win_v)[kind]
        for h in range(FIRST_SUM):
            arrived(halo_place(ref, h), halo_recv.at[kind, h])
        for part in range(chunks):
            arrived(own_win(ref, FIRST_SUM + part), loc_sem.at[kind, part])
            arrived(ref.at[pl.ds(SUMB + 2 * part, 2)], loc_sem.at[kind, chunks + part])

    window_scores(0, s_a)

    def window_pair(t, carry):
        pipelined_pair(t, window_scores, window_mix, near_m)
        return carry

    lax.fori_loop(0, n_head, window_pair, 0)
    others(1)

    def out_dest(t):
        return lax.rem(g + 2 * t + 1 - (n_head - 1) * (t // (n_head // 2)), n_head)

    def half_rows(u):
        return pl.ds(u * BLK, BLK)

    def out_to(t, u):
        dest = out_dest(t)
        return remote(
            ost.at[t, half_rows(u)], attn.at[g, half_rows(u)],
            out_send.at[2 * t + u], out_recv.at[2 * g + u], head=dest,
        )

    def finish_pair(t, carry):
        dest = out_dest(t)
        for u in range(2):
            ost[t, u * BLK : (u + 1) * BLK] = finish_block(2 * dest + u)

            @pl.when(t < n_head - 1)
            def _(u=u):
                out_to(t, u).start()

        return carry

    lax.fori_loop(0, n_head, finish_pair, 0)
    for u in range(2):
        pltpu.make_async_copy(
            ost.at[n_head - 1, half_rows(u)], attn.at[g, half_rows(u)], out_recv.at[2 * g + u]
        ).start()

    wo_copy.wait()
    for h in range(n_head):
        for u in range(2):
            arrived(attn.at[h, half_rows(u)], out_recv.at[2 * h + u])
    heads = jnp.concatenate([attn[h] for h in range(n_head)], axis=1)
    out_ref[...] = jnp.dot(heads, wo_v[...], preferred_element_type=F32).astype(BF16)

    for k in range(1, n_head):
        exchange(ks, k_send, k_recv, k, own_q).wait_send()
        exchange(vs, v_send, v_recv, k, own_q).wait_send()
        exchange(qs, q_send, q_recv, k, own_q).wait_send()
        for u in range(2):
            out_to(k - 1, u).wait_send()
    for kind in range(2):
        for h in range(FIRST_SUM):
            halo_copy(kind, h).wait_send()

        def sent(m, carry, kind=kind):
            sib_copy(kind, m, piece(kind, b, 0)).wait_send()

            @pl.when(m < n_up[kind])
            def _():
                up_copy(kind, m).wait_send()

            @pl.when(m < n_dn[kind])
            def _():
                dn_copy(kind, m).wait_send()

            return carry

        lax.fori_loop(0, chunks * n_blk // 2, sent, 0)


def on_device(n_head, n_blk, tokens, proj_weight, out_weight, pattern):
    rows = tokens.shape[1]
    n_query = pattern.shape[0]
    n_hop = SUMB * (n_blk // 8)
    n_sib = SUMB * (n_blk // 4)
    dma = pltpu.SemaphoreType.DMA
    blocks = lambda *lead: pltpu.VMEM((*lead, BLK, PAIR), BF16)
    out = pl.pallas_call(
        functools.partial(kernel, n_head, n_blk),
        out_shape=jax.ShapeDtypeStruct((rows, D), BF16),
        in_specs=[pl.BlockSpec(memory_space=pl.ANY)] * 4,
        out_specs=pl.BlockSpec(memory_space=pltpu.VMEM),
        scratch_shapes=[
            pltpu.VMEM((rows, D), BF16),
            pltpu.VMEM((n_head, D, 3 * PAIR), BF16),
            pltpu.VMEM((D, D), BF16),
            pltpu.SMEM((n_query, KSEL), jnp.int32),
            blocks(n_head, 2),
            blocks(n_head, 2),
            blocks(n_head, 2),
            blocks(SB + 2 * REACH),
            blocks(SB + 2 * REACH),
            blocks(SUMB * n_blk),
            blocks(SUMB * n_blk),
            blocks(n_query),
            pltpu.VMEM((n_query, 8, 2 * BLK), F32),
            pltpu.VMEM((n_query, SSEL * BLK, 2 * BLK), BF16),
            pltpu.VMEM((n_query, PAIR, BLK), F32),
            pltpu.VMEM((n_query, 16, 2 * BLK), F32),
            pltpu.VMEM((SSEL * BLK, 2 * BLK), F32),
            pltpu.VMEM((SSEL * BLK, 2 * BLK), F32),
            pltpu.VMEM((n_head, rows, PAIR), BF16),
            pltpu.VMEM((n_head, rows, PAIR), BF16),
            dma((3,)),
            dma((n_head,)),
            dma((n_head,)),
            dma((n_head,)),
            dma((n_head,)),
            dma((n_head,)),
            dma((n_head,)),
            dma((n_head,)),
            dma((2, n_hop)),
            dma((2, n_hop)),
            dma((2, n_hop)),
            dma((2, n_hop)),
            dma((2, n_sib)),
            dma((2, n_sib)),
            dma((2, FIRST_SUM)),
            dma((2, FIRST_SUM)),
            dma((2, SUMB)),
            dma((2 * n_head,)),
            dma((2 * n_head,)),
        ],
        compiler_params=pltpu.CompilerParams(
            collective_id=0, has_side_effects=True, vmem_limit_bytes=53 * 1024 * 1024
        ),
    )(tokens[0], proj_weight, out_weight, pattern)
    return out.reshape(1, rows, D)


def solution(mesh):
    return jax.shard_map(
        functools.partial(on_device, mesh.shape["head"], mesh.shape["blk"]),
        mesh=mesh,
        in_specs=(P(("batch", "blk"), "head", None), P(), P(), P(("batch", "blk"), None)),
        out_specs=P(("batch", "blk"), "head", None),
        check_vma=False,
    )
```
